128 devices in a mesh: mem: 8 (over y_hi, x), dom: 16 (over z, y_lo, core).
Axes of the slice: x: 4, y: 4 (y_hi: 2, y_lo: 2; y = y_hi * 2 + y_lo), z: 4, core: 2. Of those that a mesh axis runs over, the one named last changes fastest.
Arguments:
- sample_vectors_prior: float32 [32, 5, 512, 256], P('mem', None, 'dom'), may hold values from -6 to 6
- smoothing_number: float32 [5, 512, 256], P(None, 'dom'), may hold values from 0.02 to 0.2
- cross_quantity_factor: float32 [5, 5], replicated, may hold values from -0.6 to 0.6
- obs_tile: int32 [2, 2048, 1], replicated, may hold values from 0 to 15; in each aligned block of 2048 rows (0 to 2047, 2048 to 4095, ..., all dimensions but the last counted through in order) at most 256 rows name the same one
- measured_gridpoint: int32 [2, 2048], replicated, may hold values from 0 to 7904
- obs_field: int32 [2, 2048], replicated, may hold values from 0 to 4
- obs_weights: float32 [2, 2048, 4], replicated, may hold values from 0.1 to 0.5
- obs_values: float32 [2, 2048], replicated, may hold values from -8 to 8
- observation_variance: float32 [2, 2048], replicated, may hold values from 0.2 to 2
- localization: float32 [2, 16, 2048], P(None, 'dom'), may hold values from 0.001 to 0.02
Outputs:
- analysis: float32 [32, 5, 512, 256], P('mem', None, 'dom')
The draws below stay inside these ranges and needn't reach their ends.
Inputs may be any that keep to these rules, and one draw needn't show every extreme that they name: `obs_tile`: in each batch at most 256 observations share an owning tile, and in some batch some tile owns exactly 256. Local row measured_gridpoint // 255, column measured_gridpoint % 255; the four points used lie in the owning tile.
All inputs are finite; a program needn't handle non-finite values.
Results may differ from the reference program's by a relative error of at most 0.0001.
Values sent between devices are 32-bit elements; how exact they have to be, the bound alone decides.
No kernel may reach another device: no remote copies, remote signals or barrier semaphores. Data moves between devices by JAX's collectives and lax.ppermute only.
A program may use at most 128 MiB of HBM per device.

```python
import math
import jax
import jax.numpy as jnp
import numpy as np
from jax import lax

F = 5
CX = 32
GY = 256
STEPS = 2
BATCHES = 2
NOBS = 2048
TILES = 16
MEMBERS = 32
NX = 512
CAP = 256


def with_ends(values, own_key, least, largest):
    spot = [jax.random.randint(jax.random.fold_in(own_key, axis), (), 0, length) for axis, length in enumerate(values.shape)]
    widest = values.shape.index(max(values.shape))
    beside = spot[:widest] + [(spot[widest] + 1) % values.shape[widest]] + spot[widest + 1:]
    return values.at[tuple(spot)].set(least).at[tuple(beside)].set(largest)


def block_scale(key, dims, shards, smallest, high):
    def one(axis_at, shards_of):
        heights = jax.random.uniform(jax.random.fold_in(jax.random.fold_in(key, 6), axis_at), (shards_of,), jnp.float32, smallest / len(shards), high / len(shards))
        return jnp.repeat(jnp.exp(heights), dims[axis_at] // shards_of).reshape((-1,) + (1,) * (len(dims) - axis_at - 1))

    level = one(*shards[0])
    for cut in shards[1:]:
        level = level * one(*cut)
    return level


def assign_block(stream_key, own, number, rows, amount, top, most, skew):
    sequence = jax.random.permutation(stream_key, amount)
    heavy_load, common = shares(amount, rows * top, most, skew, True), shares(amount, rows * top, most, skew, False)
    places = jnp.arange(amount)

    def named(lengths, rotation):
        used = int((lengths > 0).sum())
        fixed = max(1, used // 4)
        shifted = fixed + (places - fixed + rotation * (used - fixed)) % max(1, amount - fixed)
        return jnp.zeros((amount,), jnp.int32).at[sequence[jnp.where(places < fixed, places, shifted)]].set(jnp.asarray(lengths, jnp.int32))

    lengths = jnp.where(number % 4 == 0, named(heavy_load, number // 4), named(common, number - number // 4 - 1))
    mixed = jax.random.permutation(jax.random.fold_in(own, 3), amount)
    source_of, sink = mixed[0:amount // 2 * 2:2], mixed[1:amount // 2 * 2:2]
    margin = jnp.minimum(lengths[source_of] - 1, most - lengths[sink]) // 2
    margin = jnp.where((source_of == sequence[0]) | (sink == sequence[0]) | (lengths[sink] == 0), 0, jnp.maximum(margin, 0))
    shifted = jax.random.randint(jax.random.fold_in(own, 4), (amount // 2,), 0, 1 << 20) % (margin + 1)
    lengths = lengths.at[source_of].add(-shifted).at[sink].add(shifted)
    members = jnp.searchsorted(jnp.cumsum(lengths), jnp.arange(rows * top), side="right").astype(jnp.int32)
    table = members.reshape(top, rows).T
    table = table[jax.random.permutation(jax.random.fold_in(own, 1), rows)]
    rotation = jax.random.randint(jax.random.fold_in(own, 2), (rows, 1), 0, top)
    return jnp.take_along_axis(table, (jnp.arange(top)[None, :] + rotation) % top, axis=1)


def shares(amount, total, reach, skew, full):
    portions = [(1 << 20) // math.isqrt(rank ** skew) + 1 for rank in range(1, amount + 1)]
    largest = reach if full else min(reach, max(-(-total // amount), total * portions[0] // sum(portions)))
    least = 1 if total - largest >= amount - 1 else 0
    given, rest = [largest] + [least] * (amount - 1), total - largest - least * (amount - 1)
    while rest > 0:
        candidates = [i for i in range(1, amount) if given[i] < largest] or [i for i in range(1, amount) if given[i] < reach]
        whole, left = sum([portions[i] for i in candidates]), rest
        for i in candidates:
            addition = min(reach - given[i], max(1, left * portions[i] // whole), rest)
            given[i] = given[i] + addition
            rest = rest - addition
    return np.array(given)


def normal_values(key, extent, width, bound, cuts=(), kind=jnp.bfloat16):
    drawn = jax.random.normal(key, extent, jnp.float32) * width
    if len(cuts) > 0:
        drawn = block_scale(key, extent, cuts, -0.22, 0.18) * drawn
    return jnp.clip(drawn, min=-bound, max=bound).astype(kind)


def setup_inputs(seed: int = 0) -> dict:
    key_list = jax.random.split(jax.random.key(seed), 11)
    sample_vectors_prior = normal_values(key_list[0], (MEMBERS, F, NX, GY), 1.0, 6.0, ((0, 8), (2, 16)), jnp.float32)
    smoothing_number = jnp.clip(jnp.exp(math.log(0.2) - 2.3025851 * jax.random.uniform(key_list[1], (F, NX, GY), jnp.float32) ** block_scale(key_list[1], (F, NX, GY), ((1, 16),), -0.2, 0.2)), 0.02, 0.2)
    cross_quantity_factor = normal_values(key_list[2], (F, F), 0.15, 0.6, (), jnp.float32)
    obs_tile_keys = jax.random.split(jax.random.fold_in(key_list[3], 1), BATCHES * NOBS // NOBS)
    obs_tile_turns = jax.random.permutation(jax.random.fold_in(key_list[3], 3), BATCHES * NOBS // NOBS)
    obs_tile = jax.vmap(lambda own, number: assign_block(jax.random.fold_in(key_list[3], 2), own, number, NOBS, TILES, 1, CAP, 2))(obs_tile_keys, obs_tile_turns).reshape((BATCHES, NOBS, 1))
    measured_gridpoint = with_ends(jax.random.randint(key_list[4], (BATCHES, NOBS), 0, (CX - 1) * (GY - 1)), jax.random.fold_in(key_list[4], 1), 0, ((CX - 1) * (GY - 1)) - 1).astype(jnp.int32)
    obs_field = with_ends(jax.random.randint(key_list[5], (BATCHES, NOBS), 0, F), jax.random.fold_in(key_list[5], 1), 0, F - 1).astype(jnp.int32)
    obs_weights = jnp.clip(jax.random.uniform(key_list[6], (BATCHES, NOBS, 4), jnp.float32, 0.1, 0.5), 0.1, 0.5)
    obs_values = normal_values(key_list[7], (BATCHES, NOBS), 1.5, 8.0, (), jnp.float32)
    observation_variance = jnp.clip(jnp.exp(jax.random.uniform(key_list[8], (BATCHES, NOBS), jnp.float32, math.log(0.2), math.log(2.0))), 0.2, 2.0)
    localization = jnp.clip(jnp.exp(math.log(0.02) - 2.9957322 * jax.random.uniform(key_list[9], (BATCHES, TILES, NOBS), jnp.float32) ** block_scale(key_list[9], (BATCHES, TILES, NOBS), ((1, 16),), -0.2, 0.2)), 0.001, 0.02)
    return dict(sample_vectors_prior=sample_vectors_prior, smoothing_number=smoothing_number, cross_quantity_factor=cross_quantity_factor, obs_tile=obs_tile, measured_gridpoint=measured_gridpoint, obs_field=obs_field, obs_weights=obs_weights, obs_values=obs_values, observation_variance=observation_variance, localization=localization)


def predicted_quantity(sample_vectors_prior, smoothing_number, cross_quantity_factor):
    padded = jnp.pad(sample_vectors_prior, ((0, 0), (0, 0), (1, 1), (1, 1)))
    lap = padded[:, :, 2:, 1:-1] + padded[:, :, :-2, 1:-1]
    lap = lap + padded[:, :, 1:-1, 2:] + padded[:, :, 1:-1, :-2] - 4.0 * sample_vectors_prior
    mixed = jnp.einsum('fg,mgxy->mfxy', cross_quantity_factor, sample_vectors_prior, precision=lax.Precision.HIGHEST)
    return sample_vectors_prior + smoothing_number[None] * lap + mixed

def reference(sample_vectors_prior, smoothing_number, cross_quantity_factor, obs_tile, measured_gridpoint, obs_field, obs_weights, obs_values, observation_variance, localization):
    for step_index in range(STEPS):
        sample_vectors_prior = predicted_quantity(sample_vectors_prior, smoothing_number, cross_quantity_factor)
    for batch_index in range(BATCHES):
        owner = obs_tile[batch_index, :, 0].astype(jnp.int32)
        place = measured_gridpoint[batch_index].astype(jnp.int32)
        row_local = place // (GY - 1)
        column = place % (GY - 1)
        base = obs_field[batch_index].astype(jnp.int32) * (NX * GY) + (owner * CX + row_local) * GY + column
        offsets = jnp.array([0, 1, GY, GY + 1], dtype=jnp.int32)
        points = (base[:, None] + offsets[None, :]).reshape(-1)
        flat = sample_vectors_prior.reshape(MEMBERS, F * NX * GY)
        values = jnp.take(flat, points, axis=1).reshape(MEMBERS, NOBS, 4)
        prior = lax.optimization_barrier(jnp.sum(values * obs_weights[batch_index][None], axis=-1))
        mean_prior = lax.optimization_barrier(jnp.mean(prior, axis=0))
        ensemble_spread = prior - mean_prior[None]
        variance = lax.optimization_barrier(jnp.sum(ensemble_spread * ensemble_spread, axis=0)) / (MEMBERS - 1)
        error = observation_variance[batch_index]
        total = variance + error
        gain = (obs_values[batch_index] - mean_prior)[None] / total[None] - ensemble_spread / (jnp.sqrt(total) * (jnp.sqrt(error) + jnp.sqrt(total)))[None]
        mixing = jnp.einsum('mo,to,no->tmn', ensemble_spread, localization[batch_index], gain, precision=lax.Precision.HIGHEST) / (MEMBERS - 1)
        tiles = sample_vectors_prior.reshape(MEMBERS, F, TILES, CX, GY)
        anomaly = tiles - lax.optimization_barrier(jnp.mean(tiles, axis=0))[None]
        tiles = tiles + jnp.einsum('mftxy,tmn->nftxy', anomaly, mixing, precision=lax.Precision.HIGHEST)
        sample_vectors_prior = tiles.reshape(MEMBERS, F, NX, GY)
    return sample_vectors_prior
```

```python
import jax
import jax.numpy as jnp
from jax import lax
from jax.experimental import pallas as pl
from jax.experimental.pallas import tpu as pltpu
from jax.sharding import PartitionSpec as P

F32 = jnp.float32
BF16 = jnp.bfloat16
HI = lax.Precision.HIGHEST
CAP = 256
LANES = 128


def split3(values):
    high = values.astype(BF16)
    rest = values - high.astype(F32)
    middle = rest.astype(BF16)
    low = (rest - middle.astype(F32)).astype(BF16)
    return high, middle, low


def dot_nt(a, b, precision=None):
    return lax.dot_general(
        a, b, (((1,), (1,)), ((), ())), precision=precision, preferred_element_type=F32
    )


def dot_nn(a, b, precision=None):
    return lax.dot_general(
        a, b, (((1,), (0,)), ((), ())), precision=precision, preferred_element_type=F32
    )


def iota(shape, dim):
    return lax.broadcasted_iota(jnp.int32, shape, dim)


def chosen_rows(slots, row):
    return jnp.where(slots[row : row + 1, :] == iota((CAP, LANES), 0), 1.0, 0.0).astype(BF16)


def compact_kernel(tile_ref, owner_ref, place_ref, field_ref, weight_ref, value_ref, error_ref,
                   params_ref, slots_ref, mask_ref, vals_ref):
    batches, _, count = owner_ref.shape
    chunks = count // LANES
    rows = batches * chunks
    mine = tile_ref[0]
    for b in range(batches):
        own = jnp.where(owner_ref[b] == mine, 1.0, 0.0)
        for j in range(chunks):
            mask_ref[b * chunks + j : b * chunks + j + 1, :] = own[:, j * LANES : (j + 1) * LANES]
    mask = mask_ref[...]
    mask16 = mask.astype(BF16)
    upper = jnp.where(iota((LANES, LANES), 0) <= iota((LANES, LANES), 1), 1.0, 0.0).astype(BF16)
    inside = dot_nn(mask16, upper)
    totals = dot_nn(mask16, jnp.ones((LANES, LANES), BF16)).astype(BF16)
    a, c = iota((rows, rows), 0), iota((rows, rows), 1)
    before = jnp.where((c < a) & ((c >= chunks) == (a >= chunks)), 1.0, 0.0).astype(BF16)
    rank = inside + dot_nn(before, totals) - 1.0
    slots = jnp.where(mask > 0.5, rank, -1.0).astype(jnp.int32)
    slots_ref[...] = slots
    for b in range(batches):
        place = place_ref[b : b + 1, :]
        row = ((place.astype(F32) + 0.5) * (1.0 / 255.0)).astype(jnp.int32)
        vals_ref[b, 0:1, :] = (field_ref[b : b + 1, :] * 32 + row).astype(F32)
        vals_ref[b, 1:2, :] = (place - row * 255).astype(F32)
        vals_ref[b, 2:6, :] = weight_ref[b]
        vals_ref[b, 6:7, :] = value_ref[b : b + 1, :]
        vals_ref[b, 7:8, :] = error_ref[b : b + 1, :]
        total = jnp.zeros((24, CAP), F32)
        for j in range(chunks):
            parts = split3(vals_ref[b, :, j * LANES : (j + 1) * LANES])
            total = total + dot_nt(
                jnp.concatenate([p.astype(F32) for p in parts], axis=0).astype(BF16),
                chosen_rows(slots, b * chunks + j),
            )
        params_ref[:, b * CAP : (b + 1) * CAP] = total[0:8] + total[8:16] + total[16:24]


def localize_kernel(slots_ref, loc_ref, out_ref):
    batches, tiles, count = loc_ref.shape
    chunks = count // LANES
    slots = slots_ref[...]
    for b in range(batches):
        total = jnp.zeros((3 * tiles, CAP), F32)
        for j in range(chunks):
            parts = split3(loc_ref[b, :, j * LANES : (j + 1) * LANES])
            total = total + dot_nt(
                jnp.concatenate(parts, axis=0), chosen_rows(slots, b * chunks + j)
            )
        out_ref[b] = total[:tiles] + total[tiles : 2 * tiles] + total[2 * tiles :]


TOP = 16


def forecast_kernel(cross_ref, x_ref, above_ref, below_ref, smooth_ref, params_ref,
                    out_ref, buf_ref, nxt_ref, sm_ref, fin_ref, u_ref):
    members, fields, nrows, cols = x_ref.shape
    last = TOP + nrows
    for f in range(fields):
        sm_ref[f, TOP - 1 : TOP, :] = above_ref[members, f, 1:2, :]
        sm_ref[f, TOP:last, :] = smooth_ref[f]
        sm_ref[f, last : last + 1, :] = below_ref[members, f, 0:1, :]
    for m in range(members):
        for f in range(fields):
            buf_ref[m * fields + f, TOP - 2 : TOP, :] = above_ref[m, f]
            buf_ref[m * fields + f, TOP:last, :] = x_ref[m, f]
            buf_ref[m * fields + f, last : last + 2, :] = below_ref[m, f]
    lane = iota((8, cols), 1)
    first_col, last_col = lane == 0, lane == cols - 1

    def substep(src_ref, m, base):
        own = [src_ref[m * fields + f, base : base + 8, :] for f in range(fields)]
        result = []
        for f in range(fields):
            v = own[f]
            lap = src_ref[m * fields + f, base + 1 : base + 9, :]
            lap = lap + src_ref[m * fields + f, base - 1 : base + 7, :]
            lap = lap + jnp.where(last_col, 0.0, pltpu.roll(v, cols - 1, 1))
            lap = lap + jnp.where(first_col, 0.0, pltpu.roll(v, 1, 1)) - 4.0 * v
            mixed = cross_ref[f, 0] * own[0]
            for g in range(1, fields):
                mixed = mixed + cross_ref[f, g] * own[g]
            result.append(v + sm_ref[f, base : base + 8, :] * lap + mixed)
        return result

    def member(m, carry):
        for base in range(TOP - 8, last + 8, 8):
            for f, v in enumerate(substep(buf_ref, m, base)):
                nxt_ref[m * fields + f, base : base + 8, :] = v
        for g in range(nrows // 8):
            for f, v in enumerate(substep(nxt_ref, m, TOP + 8 * g)):
                fin_ref[m, f * nrows + 8 * g : f * nrows + 8 * g + 8, :] = v
        return carry

    lax.fori_loop(0, members, member, 0)

    points = fields * nrows
    slots = params_ref.shape[1]
    spot = params_ref[0:1, :].astype(jnp.int32)
    column = params_ref[1:2, :].astype(jnp.int32)
    cid = iota((cols, slots), 0)
    left = jnp.where(cid == column, 1.0, 0.0).astype(BF16)
    right = jnp.where(cid == column + 1, 1.0, 0.0).astype(BF16)
    choice = jnp.concatenate([left, right], axis=1)
    choice = jnp.concatenate([choice, choice, choice], axis=0)
    parts = split3(fin_ref[...].reshape(members * points, cols))
    u_ref[...] = dot_nn(jnp.concatenate(parts, axis=1), choice)
    w = [params_ref[2 + k : 3 + k, :] for k in range(4)]
    acc = [jnp.zeros((8, slots), F32) for _ in range(members)]
    for i in range(points // 8):
        here = iota((8, slots), 0) + 8 * i
        at, under = here == spot, here == spot + 1
        a0 = jnp.where(at, w[0], 0.0) + jnp.where(under, w[2], 0.0)
        a1 = jnp.where(at, w[1], 0.0) + jnp.where(under, w[3], 0.0)
        for m in range(members):
            rows = slice(m * points + 8 * i, m * points + 8 * i + 8)
            acc[m] = acc[m] + a0 * u_ref[rows, 0:slots] + a1 * u_ref[rows, slots : 2 * slots]
    priors = [jnp.sum(v, axis=0, keepdims=True) for v in acc]
    halves = cols // LANES
    for g in range(nrows // 8):
        for h in range(halves):
            b = g * halves + h
            for m in range(members):
                for f in range(fields):
                    k = (m * fields + f) * 8
                    out_ref[b, k : k + 8, :] = fin_ref[
                        m, f * nrows + 8 * g : f * nrows + 8 * g + 8, h * LANES : (h + 1) * LANES
                    ]
                for q in range(slots // LANES):
                    k = members * fields * 8 + q * members + m
                    out_ref[b, k : k + 1, :] = priors[m][:, q * LANES : (q + 1) * LANES]


def load_priors(pri_ref, prior_ref):
    groups, held, _ = pri_ref.shape
    members = held * LANES // prior_ref.shape[1]
    for s in range(groups):
        for q in range(held // members):
            prior_ref[s * members : (s + 1) * members, q * LANES : (q + 1) * LANES] = pri_ref[
                s, q * members : (q + 1) * members, :
            ]


def partial_mixing(prior, value, error, loc):
    members = prior.shape[0]
    tiles = loc.shape[0]
    mean = jnp.sum(prior, axis=0, keepdims=True) * (1.0 / members)
    spread = prior - mean
    variance = jnp.sum(spread * spread, axis=0, keepdims=True) * (1.0 / (members - 1))
    error = jnp.where(error > 0.0, error, 1.0)
    total = variance + error
    root = jnp.sqrt(total)
    gain = (value - mean) / total - spread / (root * (jnp.sqrt(error) + root))
    gain = gain * (1.0 / (members - 1))
    groups = members // 8
    out = jnp.zeros((tiles * 8, LANES), F32)
    stacked = jnp.concatenate([spread] * groups, axis=0)
    group_of = iota(stacked.shape, 0) // members
    for k in range(groups):
        a = loc[:, None, :] * gain[None, 8 * k : 8 * k + 8, :]
        b = jnp.where(group_of == k, stacked, 0.0)
        out = out + dot_nt(a.reshape(tiles * 8, a.shape[2]), b, HI)
    return out.reshape(tiles, 8, LANES)


def unpack_mixing(packed_ref, members):
    packed = jnp.sum(packed_ref[...], axis=0)
    return jnp.concatenate(
        [packed[:, k * members : (k + 1) * members] for k in range(members // 8)], axis=0
    )


def first_kernel(pri_ref, params_ref, loc_ref, out_ref, prior_ref):
    load_priors(pri_ref, prior_ref)
    out_ref[...] = partial_mixing(
        prior_ref[:, 0:CAP], params_ref[6:7, 0:CAP], params_ref[7:8, 0:CAP], loc_ref[0]
    )


def second_kernel(w0_ref, pri_ref, params_ref, loc_ref, out_ref, prior_ref):
    load_priors(pri_ref, prior_ref)
    members = prior_ref.shape[0]
    w0 = unpack_mixing(w0_ref, members)
    prior = prior_ref[:, CAP : 2 * CAP]
    mean = jnp.sum(prior, axis=0, keepdims=True) * (1.0 / members)
    prior = prior + dot_nn(w0, prior - mean, HI)
    out_ref[...] = partial_mixing(
        prior, params_ref[6:7, CAP : 2 * CAP], params_ref[7:8, CAP : 2 * CAP], loc_ref[1]
    )


def apply_kernel(w0_ref, w1_ref, x_ref, out_ref):
    groups, held, _ = out_ref.shape
    own = 4
    members = groups * own
    fields = held // (own * 8)
    w0 = unpack_mixing(w0_ref, members)
    w1 = unpack_mixing(w1_ref, members)
    inv = 1.0 / members
    both = w0 + w1 + dot_nn(w1, w0 - jnp.sum(w0, axis=0, keepdims=True) * inv, HI)
    both = both - jnp.sum(both, axis=1, keepdims=True) * inv
    size = members * 8
    tall = jnp.where(iota((size, members), 0) // 8 == iota((size, members), 1), 1.0, 0.0)
    wide = jnp.where(iota((members, size), 1) // 8 == iota((members, size), 0), 1.0, 0.0)
    big = dot_nn(dot_nn(tall, both, HI), wide, HI)
    big = jnp.where(iota((size, size), 0) % 8 == iota((size, size), 1) % 8, big, 0.0)
    x = jnp.concatenate(
        [
            jnp.concatenate(
                [
                    x_ref[s, (m * fields + f) * 8 : (m * fields + f) * 8 + 8, :]
                    for s in range(groups)
                    for m in range(own)
                ],
                axis=0,
            )
            for f in range(fields)
        ],
        axis=1,
    )
    y = x + dot_nn(big, x, HI)
    for s in range(groups):
        for m in range(own):
            for f in range(fields):
                k = (m * fields + f) * 8
                n = (s * own + m) * 8
                out_ref[s, k : k + 8, :] = y[n : n + 8, f * LANES : (f + 1) * LANES]


def place_kernel(x_ref, out_ref):
    members, fields, nrows, cols = out_ref.shape
    halves = cols // LANES
    for g in range(nrows // 8):
        for h in range(halves):
            for m in range(members):
                for f in range(fields):
                    k = (m * fields + f) * 8
                    out_ref[m, f, 8 * g : 8 * g + 8, h * LANES : (h + 1) * LANES] = x_ref[
                        g * halves + h, k : k + 8, :
                    ]


VM = pltpu.VMEM
PARAMS = pltpu.CompilerParams(vmem_limit_bytes=32 << 20)


def shaped(shape, dtype=F32):
    return jax.ShapeDtypeStruct(shape, dtype)


def exchange(x, axis):
    return lax.all_to_all(x, axis, split_axis=0, concat_axis=0, tiled=False)


def on_device(x, smooth, cross, obs_tile, place, field, weights, values, error, loc):
    members, fields, nrows, cols = x.shape
    batches, count = place.shape
    tiles = lax.axis_size("dom")
    groups = lax.axis_size("mem")
    slots = batches * CAP
    mine = lax.axis_index("dom").astype(jnp.int32).reshape(1)
    smem = pl.BlockSpec(memory_space=pltpu.SMEM)
    vmem = pl.BlockSpec(memory_space=pltpu.VMEM)

    own_loc = loc[:, 0, :]
    all_loc = exchange(jnp.broadcast_to(own_loc[None], (tiles,) + own_loc.shape), "dom")

    tail = jnp.concatenate([x[:, :, nrows - 2 :], smooth[None, :, nrows - 2 :]], axis=0)
    head = jnp.concatenate([x[:, :, :2], smooth[None, :, :2]], axis=0)
    above = lax.ppermute(tail, "dom", [(i, i + 1) for i in range(tiles - 1)])
    below = lax.ppermute(head, "dom", [(i + 1, i) for i in range(tiles - 1)])

    rows = batches * count // LANES
    params, slot = pl.pallas_call(
        compact_kernel,
        out_shape=(shaped((8, slots)), shaped((rows, LANES), jnp.int32)),
        in_specs=[smem] + [vmem] * 6,
        scratch_shapes=[VM((rows, LANES), F32), VM((batches, 8, count), F32)],
        compiler_params=PARAMS,
        name="compact",
    )(mine, obs_tile.transpose(0, 2, 1), place, field, weights.transpose(0, 2, 1), values, error)

    own_rows = members * fields * 8
    prior_rows = members * slots // LANES
    blocks = nrows // 8 * (cols // LANES)
    points = fields * nrows
    sent = pl.pallas_call(
        forecast_kernel,
        out_shape=shaped((blocks, own_rows + prior_rows, LANES)),
        in_specs=[smem] + [vmem] * 5,
        scratch_shapes=[
            VM((members * fields, nrows + 32, cols), F32),
            VM((members * fields, nrows + 32, cols), F32),
            VM((fields, nrows + 32, cols), F32),
            VM((members, points, cols), F32),
            VM((members * points, 2 * slots), F32),
        ],
        compiler_params=PARAMS,
        name="forecast",
    )(cross, x, above, below, smooth, params)
    got = exchange(sent, "mem")

    loc_own = pl.pallas_call(
        localize_kernel,
        out_shape=shaped((batches, tiles, CAP)),
        compiler_params=PARAMS,
        name="localize",
    )(slot, all_loc.transpose(1, 0, 2))

    pri_spec = pl.BlockSpec((groups, prior_rows, LANES), lambda i: (0, own_rows // prior_rows, 0))
    state_spec = pl.BlockSpec((groups, own_rows, LANES), lambda i: (0, 0, 0))

    def whole(shape):
        return pl.BlockSpec(shape, lambda i: (0,) * len(shape))

    total = members * groups
    packed = (tiles, total * total // LANES, LANES)
    mix = dict(
        grid=(1,),
        out_shape=shaped(packed),
        out_specs=whole(packed),
        scratch_shapes=[VM((total, slots), F32)],
        compiler_params=PARAMS,
    )
    small = [pri_spec, whole(params.shape), whole(loc_own.shape)]
    w0 = pl.pallas_call(first_kernel, in_specs=small, name="first", **mix)(got, params, loc_own)
    w0 = exchange(w0, "dom")
    w1 = pl.pallas_call(second_kernel, in_specs=[whole(packed)] + small, name="second", **mix)(
        w0, got, params, loc_own
    )
    w1 = exchange(w1, "dom")
    back = pl.pallas_call(
        apply_kernel,
        grid=(1,),
        out_shape=shaped((groups, own_rows, LANES)),
        in_specs=[whole(packed), whole(packed), state_spec],
        out_specs=state_spec,
        compiler_params=PARAMS,
        name="apply",
    )(w0, w1, got)
    back = exchange(back, "mem")
    return pl.pallas_call(
        place_kernel, out_shape=shaped(x.shape), compiler_params=PARAMS, name="place"
    )(back)


def solution(mesh):
    placed = (
        P("mem", None, "dom", None),
        P(None, "dom", None),
        P(),
        P(),
        P(),
        P(),
        P(),
        P(),
        P(),
        P(None, "dom", None),
    )
    return jax.shard_map(
        on_device,
        mesh=mesh,
        in_specs=placed,
        out_specs=P("mem", None, "dom", None),
        check_vma=False,
    )
```

```python
import jax
import jax.numpy as jnp
from jax import lax
from jax.experimental import pallas as pl
from jax.experimental.pallas import tpu as pltpu
from jax.sharding import PartitionSpec as P

F32 = jnp.float32
BF16 = jnp.bfloat16
HI = lax.Precision.HIGHEST
CAP = 256
LANES = 128
STEPS = (2, 4, 8, 1)


def split3(values):
    high = values.astype(BF16)
    rest = values - high.astype(F32)
    middle = rest.astype(BF16)
    low = (rest - middle.astype(F32)).astype(BF16)
    return high, middle, low


def dot_nt(a, b, precision=None):
    return lax.dot_general(
        a, b, (((1,), (1,)), ((), ())), precision=precision, preferred_element_type=F32
    )


def dot_nn(a, b, precision=None):
    return lax.dot_general(
        a, b, (((1,), (0,)), ((), ())), precision=precision, preferred_element_type=F32
    )


def iota(shape, dim):
    return lax.broadcasted_iota(jnp.int32, shape, dim)


def chosen_rows(slots, row):
    return jnp.where(slots[row : row + 1, :] == iota((CAP, LANES), 0), 1.0, 0.0).astype(BF16)


def substep(src_ref, cross_ref, smooth, m, base):
    fields = len(smooth)
    cols = src_ref.shape[2]
    lane = iota((8, cols), 1)
    own = [src_ref[m * fields + f, base : base + 8, :] for f in range(fields)]
    result = []
    for f in range(fields):
        v = own[f]
        lap = src_ref[m * fields + f, base + 1 : base + 9, :]
        lap = lap + src_ref[m * fields + f, base - 1 : base + 7, :]
        lap = lap + jnp.where(lane == cols - 1, 0.0, pltpu.roll(v, cols - 1, 1))
        lap = lap + jnp.where(lane == 0, 0.0, pltpu.roll(v, 1, 1)) - 4.0 * v
        mixed = cross_ref[f, 0] * own[0]
        for g in range(1, fields):
            mixed = mixed + cross_ref[f, g] * own[g]
        result.append(v + smooth[f] * lap + mixed)
    return result


def interior_kernel(tile_ref, cross_ref, x_ref, smooth_ref, owner_ref, place_ref, field_ref,
                    weight_ref, value_ref, error_ref,
                    params_ref, slots_ref, inner_ref, strip_ref, smooth_strip_ref,
                    mask_ref, vals_ref, buf_ref, nxt_ref, sem):
    planes, nrows, cols = x_ref.shape
    members, points, _ = inner_ref.shape
    fields = points // nrows
    last = TOP + nrows
    load = pltpu.make_async_copy(x_ref, buf_ref.at[:, pl.ds(TOP, nrows), :], sem)
    load.start()
    compact(tile_ref, owner_ref, place_ref, field_ref, weight_ref, value_ref, error_ref,
            params_ref, slots_ref, mask_ref, vals_ref)
    for f in range(fields):
        smooth_strip_ref[f, 3:8, :] = smooth_ref[f, 0:5, :]
        smooth_strip_ref[f, 8:13, :] = smooth_ref[f, nrows - 5 : nrows, :]
    load.wait()
    for p in range(planes):
        strip_ref[p, 3:8, :] = buf_ref[p, TOP : TOP + 5, :]
        strip_ref[p, 8:13, :] = buf_ref[p, last - 5 : last, :]

    def member(m, carry):
        for g in range(nrows // 8):
            smooth = [smooth_ref[f, 8 * g : 8 * g + 8, :] for f in range(fields)]
            for f, v in enumerate(substep(buf_ref, cross_ref, smooth, m, TOP + 8 * g)):
                nxt_ref[m * fields + f, TOP + 8 * g : TOP + 8 * g + 8, :] = v
        for g in range(nrows // 8):
            smooth = [smooth_ref[f, 8 * g : 8 * g + 8, :] for f in range(fields)]
            for f, v in enumerate(substep(nxt_ref, cross_ref, smooth, m, TOP + 8 * g)):
                inner_ref[m, f * nrows + 8 * g : f * nrows + 8 * g + 8, :] = v
        return carry

    lax.fori_loop(0, members, member, 0)


def compact(tile_ref, owner_ref, place_ref, field_ref, weight_ref, value_ref, error_ref,
            params_ref, slots_ref, mask_ref, vals_ref):
    batches, _, count = owner_ref.shape
    chunks = count // LANES
    rows = batches * chunks
    mine = tile_ref[0]
    for b in range(batches):
        own = jnp.where(owner_ref[b] == mine, 1.0, 0.0)
        for j in range(chunks):
            mask_ref[b * chunks + j : b * chunks + j + 1, :] = own[:, j * LANES : (j + 1) * LANES]
    mask = mask_ref[...]
    mask16 = mask.astype(BF16)
    upper = jnp.where(iota((LANES, LANES), 0) <= iota((LANES, LANES), 1), 1.0, 0.0).astype(BF16)
    inside = dot_nn(mask16, upper)
    totals = dot_nn(mask16, jnp.ones((LANES, LANES), BF16)).astype(BF16)
    a, c = iota((rows, rows), 0), iota((rows, rows), 1)
    before = jnp.where((c < a) & ((c >= chunks) == (a >= chunks)), 1.0, 0.0).astype(BF16)
    rank = inside + dot_nn(before, totals) - 1.0
    slots = jnp.where(mask > 0.5, rank, -1.0).astype(jnp.int32)
    slots_ref[...] = slots
    for b in range(batches):
        place = place_ref[b : b + 1, :]
        row = ((place.astype(F32) + 0.5) * (1.0 / 255.0)).astype(jnp.int32)
        vals_ref[b, 0:1, :] = (field_ref[b : b + 1, :] * 32 + row).astype(F32)
        vals_ref[b, 1:2, :] = (place - row * 255).astype(F32)
        vals_ref[b, 2:6, :] = weight_ref[b]
        vals_ref[b, 6:7, :] = value_ref[b : b + 1, :]
        vals_ref[b, 7:8, :] = error_ref[b : b + 1, :]
        total = jnp.zeros((24, CAP), F32)
        for j in range(chunks):
            parts = split3(vals_ref[b, :, j * LANES : (j + 1) * LANES])
            total = total + dot_nt(
                jnp.concatenate([p.astype(F32) for p in parts], axis=0).astype(BF16),
                chosen_rows(slots, b * chunks + j),
            )
        params_ref[:, b * CAP : (b + 1) * CAP] = total[0:8] + total[8:16] + total[16:24]


def localize_kernel(slots_ref, near_ref, far_ref, out_ref):
    batches, tiles, _ = out_ref.shape
    slots = slots_ref[...]
    rows = slots.shape[0]
    chunks = rows // batches
    for b in range(batches):
        total = jnp.zeros((3 * tiles, CAP), F32)
        for j in range(chunks):
            at = pl.ds(b * chunks + j, tiles // 2, stride=rows)
            parts = split3(jnp.concatenate([near_ref[at, :], far_ref[at, :]], axis=0))
            total = total + dot_nt(
                jnp.concatenate(parts, axis=0), chosen_rows(slots, b * chunks + j)
            )
        out_ref[b] = total[:tiles] + total[tiles : 2 * tiles] + total[2 * tiles :]


TOP = 16


def forecast_kernel(cross_ref, inner_ref, strip_ref, smooth_strip_ref, above_ref, below_ref,
                    params_ref, out_ref, buf_ref, nxt_ref, sm_ref, fin_ref, u_ref, state_ref,
                    prior_ref, sems):
    members, points, cols = inner_ref.shape
    _, fields, _, _ = above_ref.shape
    nrows = points // fields
    fin_ref[...] = inner_ref[...]
    sm_ref[...] = smooth_strip_ref[...]
    for f in range(fields):
        sm_ref[f, 2:3, :] = above_ref[members, f, 1:2, :]
        sm_ref[f, 13:14, :] = below_ref[members, f, 0:1, :]
    for m in range(members):
        for f in range(fields):
            p = m * fields + f
            buf_ref[p, 8:24, :] = strip_ref[p]
            buf_ref[p, 9:11, :] = above_ref[m, f]
            buf_ref[p, 21:23, :] = below_ref[m, f]

    def member(m, carry):
        for h in range(2):
            smooth = [sm_ref[f, 8 * h : 8 * h + 8, :] for f in range(fields)]
            for f, v in enumerate(substep(buf_ref, cross_ref, smooth, m, 8 + 8 * h)):
                nxt_ref[m * fields + f, 8 + 8 * h : 16 + 8 * h, :] = v
        for h in range(2):
            smooth = [sm_ref[f, 8 * h : 8 * h + 8, :] for f in range(fields)]
            for f, v in enumerate(substep(nxt_ref, cross_ref, smooth, m, 8 + 8 * h)):
                at = f * nrows + h * (nrows - 2)
                fin_ref[m, at : at + 2, :] = v[3:5]
        return carry

    lax.fori_loop(0, members, member, 0)

    halves = cols // LANES
    own_rows = members * fields * 8
    for g in range(nrows // 8):
        for h in range(halves):
            for m in range(members):
                for f in range(fields):
                    k = (m * fields + f) * 8
                    state_ref[g * halves + h, k : k + 8, :] = fin_ref[
                        m, f * nrows + 8 * g : f * nrows + 8 * g + 8, h * LANES : (h + 1) * LANES
                    ]
    send = pltpu.make_async_copy(state_ref, out_ref.at[:, pl.ds(0, own_rows), :], sems.at[0])
    send.start()

    slots = params_ref.shape[1]
    spot = params_ref[0:1, :].astype(jnp.int32)
    column = params_ref[1:2, :].astype(jnp.int32)
    cid = iota((cols, slots), 0)
    left = jnp.where(cid == column, 1.0, 0.0).astype(BF16)
    right = jnp.where(cid == column + 1, 1.0, 0.0).astype(BF16)
    choice = jnp.concatenate([left, right], axis=1)
    choice = jnp.concatenate([choice, choice], axis=0)
    parts = split3(fin_ref[...].reshape(members * points, cols))[:2]
    u_ref[...] = dot_nn(jnp.concatenate(parts, axis=1), choice)
    w = [params_ref[2 + k : 3 + k, :] for k in range(4)]
    acc = [jnp.zeros((8, slots), F32) for _ in range(members)]
    for i in range(points // 8):
        here = iota((8, slots), 0) + 8 * i
        at, under = here == spot, here == spot + 1
        a0 = jnp.where(at, w[0], 0.0) + jnp.where(under, w[2], 0.0)
        a1 = jnp.where(at, w[1], 0.0) + jnp.where(under, w[3], 0.0)
        for m in range(members):
            rows = slice(m * points + 8 * i, m * points + 8 * i + 8)
            acc[m] = acc[m] + a0 * u_ref[rows, 0:slots] + a1 * u_ref[rows, slots : 2 * slots]
    for m in range(members):
        row = jnp.sum(acc[m], axis=0, keepdims=True)
        for q in range(slots // LANES):
            piece = row[:, q * LANES : (q + 1) * LANES]
            for b in range(nrows // 8 * halves):
                prior_ref[b, q * members + m : q * members + m + 1, :] = piece
    held = slots // LANES * members
    send_priors = pltpu.make_async_copy(
        prior_ref, out_ref.at[:, pl.ds(own_rows, held), :], sems.at[1]
    )
    send_priors.start()
    send.wait()
    send_priors.wait()


def load_priors(got_ref, prior_ref):
    groups, rows, _ = got_ref.shape
    total, slots = prior_ref.shape
    members = total // groups
    pieces = slots // LANES
    first = rows - pieces * members
    for s in range(groups):
        for q in range(pieces):
            k = first + q * members
            prior_ref[s * members : (s + 1) * members, q * LANES : (q + 1) * LANES] = got_ref[
                s, k : k + members, :
            ]


def distance(k):
    return sum(step for i, step in enumerate(STEPS) if (k >> i) & 1)


def partial_mixing(tile_ref, out_ref, prior, value, error, loc):
    members = prior.shape[0]
    tiles = loc.shape[0]
    mean = jnp.sum(prior, axis=0, keepdims=True) * (1.0 / members)
    spread = prior - mean
    variance = jnp.sum(spread * spread, axis=0, keepdims=True) * (1.0 / (members - 1))
    error = jnp.where(error > 0.0, error, 1.0)
    total = variance + error
    root = jnp.sqrt(total)
    gain = (value - mean) / total - spread / (root * (jnp.sqrt(error) + root))
    gain = gain * (1.0 / (members - 1))
    groups = members // 8
    out = jnp.zeros((tiles * 8, LANES), F32)
    stacked = jnp.concatenate([spread] * groups, axis=0)
    group_of = iota(stacked.shape, 0) // members
    for k in range(groups):
        a = loc[:, None, :] * gain[None, 8 * k : 8 * k + 8, :]
        b = jnp.where(group_of == k, stacked, 0.0)
        out = out + dot_nt(a.reshape(tiles * 8, a.shape[2]), b, HI)
    mine = tile_ref[0]
    for k in range(tiles):
        out_ref[mine ^ distance(k)] = out[8 * k : 8 * k + 8]


def unpack_mixing(packed_ref, members):
    packed = jnp.sum(packed_ref[...], axis=0)
    return jnp.concatenate(
        [packed[:, k * members : (k + 1) * members] for k in range(members // 8)], axis=0
    )


def first_kernel(tile_ref, pri_ref, params_ref, loc_ref, out_ref, prior_ref):
    load_priors(pri_ref, prior_ref)
    value, error = params_ref[6:7, 0:CAP], params_ref[7:8, 0:CAP]
    partial_mixing(tile_ref, out_ref, prior_ref[:, 0:CAP], value, error, loc_ref[0])


def second_kernel(tile_ref, w0_ref, pri_ref, params_ref, loc_ref, out_ref, prior_ref):
    load_priors(pri_ref, prior_ref)
    members = prior_ref.shape[0]
    w0 = unpack_mixing(w0_ref, members)
    prior = prior_ref[:, CAP : 2 * CAP]
    mean = jnp.sum(prior, axis=0, keepdims=True) * (1.0 / members)
    prior = prior + dot_nn(w0, prior - mean, HI)
    value, error = params_ref[6:7, CAP : 2 * CAP], params_ref[7:8, CAP : 2 * CAP]
    partial_mixing(tile_ref, out_ref, prior, value, error, loc_ref[1])


def apply_kernel(w0_ref, w1_ref, x_ref, out_ref):
    groups, held, _ = out_ref.shape
    own = 4
    members = groups * own
    fields = held // (own * 8)
    w0 = unpack_mixing(w0_ref, members)
    w1 = unpack_mixing(w1_ref, members)
    inv = 1.0 / members
    both = w0 + w1 + dot_nn(w1, w0 - jnp.sum(w0, axis=0, keepdims=True) * inv, HI)
    both = both - jnp.sum(both, axis=1, keepdims=True) * inv
    size = members * 8
    tall = jnp.where(iota((size, members), 0) // 8 == iota((size, members), 1), 1.0, 0.0)
    wide = jnp.where(iota((members, size), 1) // 8 == iota((members, size), 0), 1.0, 0.0)
    big = dot_nn(dot_nn(tall, both, HI), wide, HI)
    big = jnp.where(iota((size, size), 0) % 8 == iota((size, size), 1) % 8, big, 0.0)
    x = jnp.concatenate(
        [
            jnp.concatenate(
                [
                    x_ref[s, (m * fields + f) * 8 : (m * fields + f) * 8 + 8, :]
                    for s in range(groups)
                    for m in range(own)
                ],
                axis=0,
            )
            for f in range(fields)
        ],
        axis=1,
    )
    big_high, big_low, _ = split3(big)
    x_high, x_low, _ = split3(x)
    y = dot_nn(
        jnp.concatenate([big_high, big_low, big_high], axis=1),
        jnp.concatenate([x_high, x_high, x_low], axis=0),
    )
    y = x + y
    for s in range(groups):
        for m in range(own):
            for f in range(fields):
                k = (m * fields + f) * 8
                n = (s * own + m) * 8
                out_ref[s, k : k + 8, :] = y[n : n + 8, f * LANES : (f + 1) * LANES]


def place_kernel(x_ref, out_ref, sems):
    _, nrows, cols = out_ref.shape
    halves = cols // LANES
    copies = []
    for b in range(nrows // 8 * halves):
        g, h = b // halves, b % halves
        to = out_ref.at[:, pl.ds(8 * g, 8), pl.ds(h * LANES, LANES)]
        copies.append(pltpu.make_async_copy(x_ref.at[b], to, sems.at[b]))
        copies[-1].start()
    for copy in copies:
        copy.wait()


VM = pltpu.VMEM
PARAMS = pltpu.CompilerParams(vmem_limit_bytes=32 << 20)


def shaped(shape, dtype=F32):
    return jax.ShapeDtypeStruct(shape, dtype)


def swap(x, distance):
    count = lax.axis_size("dom")
    return lax.ppermute(x, "dom", [(i, i ^ distance) for i in range(count)])


def exchange(x, axis):
    return lax.all_to_all(x, axis, split_axis=0, concat_axis=0, tiled=False)


def on_device(x, smooth, cross, obs_tile, place, field, weights, values, error, loc):
    members, fields, nrows, cols = x.shape
    batches, count = place.shape
    tiles = lax.axis_size("dom")
    groups = lax.axis_size("mem")
    slots = batches * CAP
    mine = lax.axis_index("dom").astype(jnp.int32).reshape(1)
    smem = pl.BlockSpec(memory_space=pltpu.SMEM)
    vmem = pl.BlockSpec(memory_space=pltpu.VMEM)

    rows = batches * count // LANES
    held = loc.reshape(rows, LANES)
    held = jnp.concatenate([held, swap(held, STEPS[0])], axis=0)

    tail = jnp.concatenate([x[:, :, nrows - 2 :], smooth[None, :, nrows - 2 :]], axis=0)
    head = jnp.concatenate([x[:, :, :2], smooth[None, :, :2]], axis=0)
    above = lax.ppermute(tail, "dom", [(i, i + 1) for i in range(tiles - 1)])
    below = lax.ppermute(head, "dom", [(i + 1, i) for i in range(tiles - 1)])

    points = fields * nrows
    planes = members * fields
    hbm = pl.BlockSpec(memory_space=pltpu.HBM)
    params, slot, inner, strip, smooth_strip = pl.pallas_call(
        interior_kernel,
        out_shape=(
            shaped((8, slots)),
            shaped((rows, LANES), jnp.int32),
            shaped((members, points, cols)),
            shaped((planes, 16, cols)),
            shaped((fields, 16, cols)),
        ),
        in_specs=[smem, smem, hbm] + [vmem] * 7,
        scratch_shapes=[
            VM((rows, LANES), F32),
            VM((batches, 8, count), F32),
            VM((planes, nrows + 32, cols), F32),
            VM((planes, nrows + 32, cols), F32),
            pltpu.SemaphoreType.DMA,
        ],
        compiler_params=PARAMS,
        name="interior",
    )(
        mine, cross, pltpu.with_memory_space_constraint(x.reshape(planes, nrows, cols), pltpu.HBM), smooth, obs_tile.transpose(0, 2, 1), place,
        field, weights.transpose(0, 2, 1), values, error,
    )

    held, above, below, params = lax.optimization_barrier((held, above, below, params))
    held = jnp.concatenate([held, swap(held, STEPS[1])], axis=0)

    own_rows = members * fields * 8
    prior_rows = members * slots // LANES
    blocks = nrows // 8 * (cols // LANES)
    sent = pl.pallas_call(
        forecast_kernel,
        out_shape=shaped((blocks, own_rows + prior_rows, LANES)),
        in_specs=[smem] + [vmem] * 6,
        out_specs=hbm,
        scratch_shapes=[
            VM((planes, 32, cols), F32),
            VM((planes, 32, cols), F32),
            VM((fields, 16, cols), F32),
            VM((members, points, cols), F32),
            VM((members * points, 2 * slots), F32),
            VM((blocks, own_rows, LANES), F32),
            VM((blocks, prior_rows, LANES), F32),
            pltpu.SemaphoreType.DMA((2,)),
        ],
        compiler_params=PARAMS,
        name="forecast",
    )(cross, inner, strip, smooth_strip, above, below, params)
    held, sent = lax.optimization_barrier((held, sent))
    got = exchange(sent, "mem")
    held = jnp.concatenate([held, swap(held, STEPS[2])], axis=0)

    loc_own = pl.pallas_call(
        localize_kernel,
        out_shape=shaped((batches, tiles, CAP)),
        compiler_params=PARAMS,
        name="localize",
    )(slot, held, swap(held, STEPS[3]))

    total = members * groups
    mix = dict(
        out_shape=shaped((tiles, total * total // LANES, LANES)),
        scratch_shapes=[VM((total, slots), F32)],
        compiler_params=PARAMS,
    )
    w0 = pl.pallas_call(first_kernel, in_specs=[smem] + [vmem] * 3, name="first", **mix)(
        mine, got, params, loc_own
    )
    w0 = exchange(w0, "dom")
    w1 = pl.pallas_call(second_kernel, in_specs=[smem] + [vmem] * 4, name="second", **mix)(
        mine, w0, got, params, loc_own
    )
    w1 = exchange(w1, "dom")
    back = pl.pallas_call(
        apply_kernel,
        out_shape=shaped((groups, own_rows, LANES)),
        compiler_params=PARAMS,
        name="apply",
    )(w0, w1, got)
    back = exchange(back, "mem")
    back = pl.pallas_call(
        place_kernel,
        out_shape=shaped((planes, nrows, cols)),
        out_specs=hbm,
        scratch_shapes=[pltpu.SemaphoreType.DMA((blocks,))],
        compiler_params=PARAMS,
        name="place",
    )(back.reshape(blocks, planes, 8, LANES))
    return back.reshape(x.shape)


def solution(mesh):
    placed = (
        P("mem", None, "dom", None),
        P(None, "dom", None),
        P(),
        P(),
        P(),
        P(),
        P(),
        P(),
        P(),
        P(None, "dom", None),
    )
    return jax.shard_map(
        on_device,
        mesh=mesh,
        in_specs=placed,
        out_specs=P("mem", None, "dom", None),
        check_vma=False,
    )
```

```python
import jax
import jax.numpy as jnp
from jax import lax
from jax.experimental import pallas as pl
from jax.experimental.pallas import tpu as pltpu
from jax.sharding import PartitionSpec as P

F32 = jnp.float32
BF16 = jnp.bfloat16
HI = lax.Precision.HIGHEST
CAP = 256
LANES = 128
STEPS = (2, 4, 8, 1)


def split3(values):
    high = values.astype(BF16)
    rest = values - high.astype(F32)
    middle = rest.astype(BF16)
    low = (rest - middle.astype(F32)).astype(BF16)
    return high, middle, low


def dot_nt(a, b, precision=None):
    return lax.dot_general(
        a, b, (((1,), (1,)), ((), ())), precision=precision, preferred_element_type=F32
    )


def dot_nn(a, b, precision=None):
    return lax.dot_general(
        a, b, (((1,), (0,)), ((), ())), precision=precision, preferred_element_type=F32
    )


def iota(shape, dim):
    return lax.broadcasted_iota(jnp.int32, shape, dim)


def chosen_rows(slots, row):
    here = slots[row : row + 1, :] == iota((CAP, LANES), 0)
    return jnp.where(here, 1.0, 0.0).astype(BF16)


def substep(src_ref, cross_ref, smooth, m, base):
    fields = len(smooth)
    cols = src_ref.shape[2]
    lane = iota((8, cols), 1)
    own = [src_ref[m * fields + f, base : base + 8, :] for f in range(fields)]
    result = []
    for f in range(fields):
        v = own[f]
        lap = src_ref[m * fields + f, base + 1 : base + 9, :]
        lap = lap + src_ref[m * fields + f, base - 1 : base + 7, :]
        lap = lap + jnp.where(lane == cols - 1, 0.0, pltpu.roll(v, cols - 1, 1))
        lap = lap + jnp.where(lane == 0, 0.0, pltpu.roll(v, 1, 1)) - 4.0 * v
        mixed = cross_ref[f, 0] * own[0]
        for g in range(1, fields):
            mixed = mixed + cross_ref[f, g] * own[g]
        result.append(v + smooth[f] * lap + mixed)
    return result


def edge_kernel(x_ref, smooth_ref, cross_ref, tail_ref, head_ref, cross_out_ref,
                tail_x, head_x, tail_s, head_s, sems):
    planes, nrows, _ = x_ref.shape
    fields = smooth_ref.shape[0]
    top, bottom = pl.ds(0, 8), pl.ds(nrows - 8, 8)
    copies = [
        pltpu.make_async_copy(x_ref.at[:, bottom, :], tail_x, sems.at[0]),
        pltpu.make_async_copy(smooth_ref.at[:, bottom, :], tail_s, sems.at[1]),
        pltpu.make_async_copy(x_ref.at[:, top, :], head_x, sems.at[2]),
        pltpu.make_async_copy(smooth_ref.at[:, top, :], head_s, sems.at[3]),
        pltpu.make_async_copy(cross_ref, cross_out_ref, sems.at[4]),
    ]
    for copy in copies:
        copy.start()
    for copy in copies:
        copy.wait()
    for p in range(planes):
        tail_ref[p] = tail_x[p, 6:8, :]
        head_ref[p] = head_x[p, 0:2, :]
    for f in range(fields):
        tail_ref[planes + f] = tail_s[f, 6:8, :]
        head_ref[planes + f] = head_s[f, 0:2, :]


def interior_kernel(tile_ref, cross_ref, x_ref, smooth_ref, owner_ref, place_ref, field_ref,
                    weight_ref, value_ref, error_ref,
                    params_ref, slots_ref, inner_ref, strip_ref, smooth_strip_ref,
                    mask_ref, vals_ref, buf_ref, nxt_ref, sem):
    planes, nrows, cols = x_ref.shape
    members, points, _ = inner_ref.shape
    fields = points // nrows
    last = TOP + nrows
    load = pltpu.make_async_copy(x_ref, buf_ref.at[:, pl.ds(TOP, nrows), :], sem)
    load.start()
    compact(tile_ref, owner_ref, place_ref, field_ref, weight_ref, value_ref, error_ref,
            params_ref, slots_ref, mask_ref, vals_ref)
    for f in range(fields):
        smooth_strip_ref[f, 3:8, :] = smooth_ref[f, 0:5, :]
        smooth_strip_ref[f, 8:13, :] = smooth_ref[f, nrows - 5 : nrows, :]
    load.wait()
    for p in range(planes):
        strip_ref[p, 3:8, :] = buf_ref[p, TOP : TOP + 5, :]
        strip_ref[p, 8:13, :] = buf_ref[p, last - 5 : last, :]

    def member(m, carry):
        for g in range(nrows // 8):
            smooth = [smooth_ref[f, 8 * g : 8 * g + 8, :] for f in range(fields)]
            for f, v in enumerate(substep(buf_ref, cross_ref, smooth, m, TOP + 8 * g)):
                nxt_ref[m * fields + f, TOP + 8 * g : TOP + 8 * g + 8, :] = v
        for g in range(nrows // 8):
            smooth = [smooth_ref[f, 8 * g : 8 * g + 8, :] for f in range(fields)]
            for f, v in enumerate(substep(nxt_ref, cross_ref, smooth, m, TOP + 8 * g)):
                inner_ref[m, f * nrows + 8 * g : f * nrows + 8 * g + 8, :] = v
        return carry

    lax.fori_loop(0, members, member, 0, unroll=True)


def compact(tile_ref, owner_ref, place_ref, field_ref, weight_ref, value_ref, error_ref,
            params_ref, slots_ref, mask_ref, vals_ref):
    batches, _, count = owner_ref.shape
    chunks = count // LANES
    rows = batches * chunks
    mine = tile_ref[0]
    for b in range(batches):
        own = jnp.where(owner_ref[b] == mine, 1.0, 0.0)
        for j in range(chunks):
            mask_ref[b * chunks + j : b * chunks + j + 1, :] = own[:, j * LANES : (j + 1) * LANES]
    mask = mask_ref[...]
    mask16 = mask.astype(BF16)
    upper = jnp.where(iota((LANES, LANES), 0) <= iota((LANES, LANES), 1), 1.0, 0.0).astype(BF16)
    inside = dot_nn(mask16, upper)
    totals = dot_nn(mask16, jnp.ones((LANES, LANES), BF16)).astype(BF16)
    a, c = iota((rows, rows), 0), iota((rows, rows), 1)
    before = jnp.where((c < a) & ((c >= chunks) == (a >= chunks)), 1.0, 0.0).astype(BF16)
    rank = inside + dot_nn(before, totals) - 1.0
    slots = jnp.where(mask > 0.5, rank, -1.0).astype(jnp.int32)
    slots_ref[...] = slots
    for b in range(batches):
        place = place_ref[b : b + 1, :]
        row = ((place.astype(F32) + 0.5) * (1.0 / 255.0)).astype(jnp.int32)
        vals_ref[b, 0:1, :] = (field_ref[b : b + 1, :] * 32 + row).astype(F32)
        vals_ref[b, 1:2, :] = (place - row * 255).astype(F32)
        vals_ref[b, 2:6, :] = weight_ref[b]
        vals_ref[b, 6:7, :] = value_ref[b : b + 1, :]
        vals_ref[b, 7:8, :] = error_ref[b : b + 1, :]
        total = jnp.zeros((24, CAP), F32)
        for j in range(chunks):
            parts = split3(vals_ref[b, :, j * LANES : (j + 1) * LANES])
            total = total + dot_nt(
                jnp.concatenate([p.astype(F32) for p in parts], axis=0).astype(BF16),
                chosen_rows(slots, b * chunks + j),
            )
        params_ref[:, b * CAP : (b + 1) * CAP] = total[0:8] + total[8:16] + total[16:24]


def localize_kernel(slots_ref, near_ref, far_ref, out_ref):
    batches, tiles, _ = out_ref.shape
    slots = slots_ref[...]
    rows = slots.shape[0]
    chunks = rows // batches
    for b in range(batches):
        total = jnp.zeros((3 * tiles, CAP), F32)
        for j in range(chunks):
            at = pl.ds(b * chunks + j, tiles // 2, stride=rows)
            parts = split3(jnp.concatenate([near_ref[at, :], far_ref[at, :]], axis=0))
            total = total + dot_nt(
                jnp.concatenate(parts, axis=0), chosen_rows(slots, b * chunks + j)
            )
        out_ref[b] = total[:tiles] + total[tiles : 2 * tiles] + total[2 * tiles :]


TOP = 16


def forecast_kernel(cross_ref, inner_ref, strip_ref, smooth_strip_ref, above_ref, below_ref,
                    params_ref, out_ref, buf_ref, nxt_ref, sm_ref, fin_ref, u_ref, state_ref,
                    prior_ref, sems):
    members, points, cols = inner_ref.shape
    fields = smooth_strip_ref.shape[0]
    nrows = points // fields
    planes = members * fields
    fin_ref[...] = inner_ref[...]
    sm_ref[...] = smooth_strip_ref[...]
    for f in range(fields):
        sm_ref[f, 2:3, :] = above_ref[planes + f, 1:2, :]
        sm_ref[f, 13:14, :] = below_ref[planes + f, 0:1, :]
    for p in range(planes):
        buf_ref[p, 8:24, :] = strip_ref[p]
        buf_ref[p, 9:11, :] = above_ref[p]
        buf_ref[p, 21:23, :] = below_ref[p]

    def member(m, carry):
        for h in range(2):
            smooth = [sm_ref[f, 8 * h : 8 * h + 8, :] for f in range(fields)]
            for f, v in enumerate(substep(buf_ref, cross_ref, smooth, m, 8 + 8 * h)):
                nxt_ref[m * fields + f, 8 + 8 * h : 16 + 8 * h, :] = v
        for h in range(2):
            smooth = [sm_ref[f, 8 * h : 8 * h + 8, :] for f in range(fields)]
            for f, v in enumerate(substep(nxt_ref, cross_ref, smooth, m, 8 + 8 * h)):
                at = f * nrows + h * (nrows - 2)
                fin_ref[m, at : at + 2, :] = v[3:5]
        return carry

    lax.fori_loop(0, members, member, 0, unroll=True)

    halves = cols // LANES
    own_rows = members * fields * 8
    for g in range(nrows // 8):
        for h in range(halves):
            for m in range(members):
                for f in range(fields):
                    k = (m * fields + f) * 8
                    state_ref[g * halves + h, k : k + 8, :] = fin_ref[
                        m, f * nrows + 8 * g : f * nrows + 8 * g + 8, h * LANES : (h + 1) * LANES
                    ]
    send = pltpu.make_async_copy(state_ref, out_ref.at[:, pl.ds(0, own_rows), :], sems.at[0])
    send.start()

    slots = params_ref.shape[1]
    spot = params_ref[0:1, :].astype(jnp.int32)
    column = params_ref[1:2, :].astype(jnp.int32)
    cid = iota((cols, slots), 0)
    left = jnp.where(cid == column, 1.0, 0.0).astype(BF16)
    right = jnp.where(cid == column + 1, 1.0, 0.0).astype(BF16)
    choice = jnp.concatenate([left, right], axis=1)
    choice = jnp.concatenate([choice, choice], axis=0)
    parts = split3(fin_ref[...].reshape(members * points, cols))[:2]
    u_ref[...] = dot_nn(jnp.concatenate(parts, axis=1), choice)
    w = [params_ref[2 + k : 3 + k, :] for k in range(4)]
    acc = [jnp.zeros((8, slots), F32) for _ in range(members)]
    for i in range(points // 8):
        here = iota((8, slots), 0) + 8 * i
        at, under = here == spot, here == spot + 1
        a0 = jnp.where(at, w[0], 0.0) + jnp.where(under, w[2], 0.0)
        a1 = jnp.where(at, w[1], 0.0) + jnp.where(under, w[3], 0.0)
        for m in range(members):
            rows = slice(m * points + 8 * i, m * points + 8 * i + 8)
            acc[m] = acc[m] + a0 * u_ref[rows, 0:slots] + a1 * u_ref[rows, slots : 2 * slots]
    for m in range(members):
        row = jnp.sum(acc[m], axis=0, keepdims=True)
        for q in range(slots // LANES):
            piece = row[:, q * LANES : (q + 1) * LANES]
            for b in range(nrows // 8 * halves):
                prior_ref[b, q * members + m : q * members + m + 1, :] = piece
    held = slots // LANES * members
    send_priors = pltpu.make_async_copy(
        prior_ref, out_ref.at[:, pl.ds(own_rows, held), :], sems.at[1]
    )
    send_priors.start()
    send.wait()
    send_priors.wait()


def load_priors(got_ref, prior_ref, batch):
    groups, rows, _ = got_ref.shape
    total = prior_ref.shape[0]
    members = total // groups
    pieces = CAP // LANES
    first = rows - (2 - batch) * pieces * members
    for s in range(groups):
        for q in range(pieces):
            k = first + q * members
            prior_ref[s * members : (s + 1) * members, q * LANES : (q + 1) * LANES] = got_ref[
                s, k : k + members, :
            ]
    return prior_ref[...]


def distance(k):
    return sum(step for i, step in enumerate(STEPS) if (k >> i) & 1)


def partial_mixing(tile_ref, out_ref, prior, value, error, loc):
    members = prior.shape[0]
    tiles = loc.shape[0]
    mean = jnp.sum(prior, axis=0, keepdims=True) * (1.0 / members)
    spread = prior - mean
    variance = jnp.sum(spread * spread, axis=0, keepdims=True) * (1.0 / (members - 1))
    error = jnp.where(error > 0.0, error, 1.0)
    total = variance + error
    root = jnp.sqrt(total)
    gain = (value - mean) / total - spread / (root * (jnp.sqrt(error) + root))
    gain = gain * (1.0 / (members - 1))
    groups = members // 8
    high, low, _ = split3(jnp.concatenate([spread] * groups, axis=0))
    group_of = iota(high.shape, 0) // members
    left, right = [], []
    for k in range(groups):
        a = (loc[:, None, :] * gain[None, 8 * k : 8 * k + 8, :]).reshape(tiles * 8, loc.shape[1])
        a_high, a_low, _ = split3(a)
        b_high, b_low = [
            jnp.where(group_of == k, p.astype(F32), 0.0).astype(BF16) for p in (high, low)
        ]
        left += [a_high, a_low, a_high]
        right += [b_high, b_high, b_low]
    out = dot_nt(jnp.concatenate(left, axis=1), jnp.concatenate(right, axis=1))
    mine = tile_ref[0]
    for k in range(tiles):
        out_ref[mine ^ distance(k)] = out[8 * k : 8 * k + 8]


def unpack_mixing(packed, members):
    return jnp.concatenate(
        [packed[:, k * members : (k + 1) * members] for k in range(members // 8)], axis=0
    )


def first_kernel(tile_ref, pri_ref, params_ref, loc_ref, out_ref, prior_ref):
    value, error = params_ref[6:7, 0:CAP], params_ref[7:8, 0:CAP]
    partial_mixing(tile_ref, out_ref, load_priors(pri_ref, prior_ref, 0), value, error, loc_ref[0])


def second_kernel(tile_ref, w0_ref, pri_ref, params_ref, loc_ref, out_ref, prior_ref):
    prior = load_priors(pri_ref, prior_ref, 1)
    members = prior_ref.shape[0]
    w0 = unpack_mixing(jnp.sum(w0_ref[...], axis=0), members)
    mean = jnp.sum(prior, axis=0, keepdims=True) * (1.0 / members)
    prior = prior + dot_nn(w0, prior - mean, HI)
    value, error = params_ref[6:7, CAP : 2 * CAP], params_ref[7:8, CAP : 2 * CAP]
    partial_mixing(tile_ref, out_ref, prior, value, error, loc_ref[1])


def apply_kernel(w0_ref, w1_ref, got_ref, out_ref):
    groups, held, _ = out_ref.shape
    w0_sum, w1_sum = jnp.sum(w0_ref[...], axis=0), jnp.sum(w1_ref[...], axis=0)
    members = groups * 4
    own = members // groups
    fields = held // (own * 8)
    w0, w1 = unpack_mixing(w0_sum, members), unpack_mixing(w1_sum, members)
    inv = 1.0 / members
    w = w0 + w1 + dot_nn(w1, w0 - jnp.sum(w0, axis=0, keepdims=True) * inv, HI)
    w = w - jnp.sum(w, axis=1, keepdims=True) * inv
    size = members * 8
    pieces = jnp.concatenate([p.astype(F32) for p in split3(w)[:2]], axis=1).astype(BF16)
    tall = jnp.where(iota((size, members), 0) // 8 == iota((size, members), 1), 1.0, 0.0)
    wide = jnp.where(
        iota((2 * members, 2 * size), 1) // 8 == iota((2 * members, 2 * size), 0), 1.0, 0.0
    )
    big = dot_nn(dot_nn(tall.astype(BF16), pieces).astype(BF16), wide.astype(BF16))
    same = iota((size, 2 * size), 0) % 8 == iota((size, 2 * size), 1) % 8
    big = jnp.where(same, big, 0.0).astype(BF16)
    for f in range(fields):
        x = jnp.concatenate(
            [
                got_ref[s, (m * fields + f) * 8 : (m * fields + f) * 8 + 8, :]
                for s in range(groups)
                for m in range(own)
            ],
            axis=0,
        )
        high, low, _ = split3(x)
        y = dot_nn(big, jnp.concatenate([high, high], axis=0)) + dot_nn(big[:, :size], low)
        y = x + y
        for s in range(groups):
            for m in range(own):
                k = (m * fields + f) * 8
                n = (s * own + m) * 8
                out_ref[s, k : k + 8, :] = y[n : n + 8]


def place_kernel(x_ref, out_ref, sems):
    _, nrows, cols = out_ref.shape
    halves = cols // LANES
    copies = []
    for b in range(nrows // 8 * halves):
        g, h = b // halves, b % halves
        to = out_ref.at[:, pl.ds(8 * g, 8), pl.ds(h * LANES, LANES)]
        copies.append(pltpu.make_async_copy(x_ref.at[b], to, sems.at[b]))
        copies[-1].start()
    for copy in copies:
        copy.wait()


VM = pltpu.VMEM
PARAMS = pltpu.CompilerParams(vmem_limit_bytes=32 << 20)


def shaped(shape, dtype=F32):
    return jax.ShapeDtypeStruct(shape, dtype)


def swap(x, distance):
    count = lax.axis_size("dom")
    return lax.ppermute(x, "dom", [(i, i ^ distance) for i in range(count)])


def exchange(x, axis):
    return lax.all_to_all(x, axis, split_axis=0, concat_axis=0, tiled=False)


def on_device(x, smooth, cross, obs_tile, place, field, weights, values, error, loc):
    members, fields, nrows, cols = x.shape
    batches, count = place.shape
    tiles = lax.axis_size("dom")
    groups = lax.axis_size("mem")
    slots = batches * CAP
    mine = lax.axis_index("dom").astype(jnp.int32).reshape(1)
    smem = pl.BlockSpec(memory_space=pltpu.SMEM)
    vmem = pl.BlockSpec(memory_space=pltpu.VMEM)

    rows = batches * count // LANES
    held = loc.reshape(rows, LANES)
    held = jnp.concatenate([held, swap(held, STEPS[0])], axis=0)

    planes = members * fields
    hbm = pl.BlockSpec(memory_space=pltpu.HBM)
    x_hbm = pltpu.with_memory_space_constraint(x.reshape(planes, nrows, cols), pltpu.HBM)
    tail, head, cross = pl.pallas_call(
        edge_kernel,
        out_shape=(
            shaped((planes + fields, 2, cols)),
            shaped((planes + fields, 2, cols)),
            shaped(cross.shape),
        ),
        in_specs=[hbm] * 3,
        scratch_shapes=[
            VM((planes, 8, cols), F32),
            VM((planes, 8, cols), F32),
            VM((fields, 8, cols), F32),
            VM((fields, 8, cols), F32),
            pltpu.SemaphoreType.DMA((5,)),
        ],
        compiler_params=PARAMS,
        name="edges",
    )(
        x_hbm,
        pltpu.with_memory_space_constraint(smooth, pltpu.HBM),
        pltpu.with_memory_space_constraint(cross, pltpu.HBM),
    )
    above = lax.ppermute(tail, "dom", [(i, i + 1) for i in range(tiles - 1)])
    below = lax.ppermute(head, "dom", [(i + 1, i) for i in range(tiles - 1)])

    points = fields * nrows
    params, slot, inner, strip, smooth_strip = pl.pallas_call(
        interior_kernel,
        out_shape=(
            shaped((8, slots)),
            shaped((rows, LANES), jnp.int32),
            shaped((members, points, cols)),
            shaped((planes, 16, cols)),
            shaped((fields, 16, cols)),
        ),
        in_specs=[smem, smem, hbm] + [vmem] * 7,
        scratch_shapes=[
            VM((rows, LANES), F32),
            VM((batches, 8, count), F32),
            VM((planes, nrows + 32, cols), F32),
            VM((planes, nrows + 32, cols), F32),
            pltpu.SemaphoreType.DMA,
        ],
        compiler_params=PARAMS,
        name="interior",
    )(
        mine, cross, x_hbm, smooth, obs_tile.transpose(0, 2, 1), place,
        field, weights.transpose(0, 2, 1), values, error,
    )

    held, above, below, params = lax.optimization_barrier((held, above, below, params))
    held = jnp.concatenate([held, swap(held, STEPS[1])], axis=0)

    own_rows = members * fields * 8
    prior_rows = members * slots // LANES
    blocks = nrows // 8 * (cols // LANES)
    sent = pl.pallas_call(
        forecast_kernel,
        out_shape=shaped((blocks, own_rows + prior_rows, LANES)),
        in_specs=[smem] + [vmem] * 6,
        out_specs=hbm,
        scratch_shapes=[
            VM((planes, 32, cols), F32),
            VM((planes, 32, cols), F32),
            VM((fields, 16, cols), F32),
            VM((members, points, cols), F32),
            VM((members * points, 2 * slots), F32),
            VM((blocks, own_rows, LANES), F32),
            VM((blocks, prior_rows, LANES), F32),
            pltpu.SemaphoreType.DMA((2,)),
        ],
        compiler_params=PARAMS,
        name="forecast",
    )(cross, inner, strip, smooth_strip, above, below, params)
    held, sent = lax.optimization_barrier((held, sent))
    got = exchange(sent, "mem")
    held = jnp.concatenate([held, swap(held, STEPS[2])], axis=0)

    loc_own = pl.pallas_call(
        localize_kernel,
        out_shape=shaped((batches, tiles, CAP)),
        compiler_params=PARAMS,
        name="localize",
    )(slot, held, swap(held, STEPS[3]))

    total = members * groups
    mix = dict(
        out_shape=shaped((tiles, total * total // LANES, LANES)),
        scratch_shapes=[VM((total, CAP), F32)],
        compiler_params=PARAMS,
    )
    w0 = pl.pallas_call(first_kernel, in_specs=[smem] + [vmem] * 3, name="first", **mix)(
        mine, got, params, loc_own
    )
    w0 = exchange(w0, "dom")
    w1 = pl.pallas_call(second_kernel, in_specs=[smem] + [vmem] * 4, name="second", **mix)(
        mine, w0, got, params, loc_own
    )
    w1 = exchange(w1, "dom")
    back = pl.pallas_call(
        apply_kernel,
        out_shape=shaped((groups, own_rows, LANES)),
        compiler_params=PARAMS,
        name="apply",
    )(w0, w1, got)
    back = exchange(back, "mem")
    back = pl.pallas_call(
        place_kernel,
        out_shape=shaped((planes, nrows, cols)),
        out_specs=hbm,
        scratch_shapes=[pltpu.SemaphoreType.DMA((blocks,))],
        compiler_params=PARAMS,
        name="place",
    )(back.reshape(blocks, planes, 8, LANES))
    return back.reshape(x.shape)


def solution(mesh):
    placed = (
        P("mem", None, "dom", None),
        P(None, "dom", None),
        P(),
        P(),
        P(),
        P(),
        P(),
        P(),
        P(),
        P(None, "dom", None),
    )
    return jax.shard_map(
        on_device,
        mesh=mesh,
        in_specs=placed,
        out_specs=P("mem", None, "dom", None),
        check_vma=False,
    )
```

```python
import jax
import jax.numpy as jnp
from jax import lax
from jax.experimental import pallas as pl
from jax.experimental.pallas import tpu as pltpu
from jax.sharding import PartitionSpec as P

F32 = jnp.float32
BF16 = jnp.bfloat16
HI = lax.Precision.HIGHEST
CAP = 256
LANES = 128
STEPS = (2, 4, 8, 1)


def split3(values):
    high = values.astype(BF16)
    rest = values - high.astype(F32)
    middle = rest.astype(BF16)
    low = (rest - middle.astype(F32)).astype(BF16)
    return high, middle, low


def dot_nt(a, b, precision=None):
    return lax.dot_general(
        a, b, (((1,), (1,)), ((), ())), precision=precision, preferred_element_type=F32
    )


def dot_nn(a, b, precision=None):
    return lax.dot_general(
        a, b, (((1,), (0,)), ((), ())), precision=precision, preferred_element_type=F32
    )


def iota(shape, dim):
    return lax.broadcasted_iota(jnp.int32, shape, dim)


def chosen_rows(slots, row):
    here = slots[row : row + 1, :] == iota((CAP, LANES), 0)
    return jnp.where(here, 1.0, 0.0).astype(BF16)


def substep(src_ref, cross_ref, smooth, m, base):
    fields = len(smooth)
    cols = src_ref.shape[2]
    lane = iota((8, cols), 1)
    own = [src_ref[m * fields + f, base : base + 8, :] for f in range(fields)]
    result = []
    for f in range(fields):
        v = own[f]
        lap = src_ref[m * fields + f, base + 1 : base + 9, :]
        lap = lap + src_ref[m * fields + f, base - 1 : base + 7, :]
        lap = lap + jnp.where(lane == cols - 1, 0.0, pltpu.roll(v, cols - 1, 1))
        lap = lap + jnp.where(lane == 0, 0.0, pltpu.roll(v, 1, 1)) - 4.0 * v
        mixed = cross_ref[f, 0] * own[0]
        for g in range(1, fields):
            mixed = mixed + cross_ref[f, g] * own[g]
        result.append(v + smooth[f] * lap + mixed)
    return result


def edge_kernel(tile_ref, x_ref, smooth_ref, cross_ref, first_ref, second_ref, cross_out_ref,
                tail_x, head_x, tail_s, head_s, sems):
    planes, nrows, _ = x_ref.shape
    fields = smooth_ref.shape[0]
    top, bottom = pl.ds(0, 8), pl.ds(nrows - 8, 8)
    copies = [
        pltpu.make_async_copy(x_ref.at[:, bottom, :], tail_x, sems.at[0]),
        pltpu.make_async_copy(smooth_ref.at[:, bottom, :], tail_s, sems.at[1]),
        pltpu.make_async_copy(x_ref.at[:, top, :], head_x, sems.at[2]),
        pltpu.make_async_copy(smooth_ref.at[:, top, :], head_s, sems.at[3]),
        pltpu.make_async_copy(cross_ref, cross_out_ref, sems.at[4]),
    ]
    for copy in copies:
        copy.start()
    for copy in copies:
        copy.wait()
    even = tile_ref[0] % 2 == 0
    for p in range(planes + fields):
        if p < planes:
            tail, head = tail_x[p, 6:8, :], head_x[p, 0:2, :]
        else:
            tail, head = tail_s[p - planes, 6:8, :], head_s[p - planes, 0:2, :]
        first_ref[p] = jnp.where(even, tail, head)
        second_ref[p] = jnp.where(even, head, tail)


def interior_kernel(tile_ref, cross_ref, x_ref, smooth_ref, owner_ref, place_ref, field_ref,
                    weight_ref, value_ref, error_ref,
                    params_ref, slots_ref, inner_ref, strip_ref, smooth_strip_ref,
                    mask_ref, vals_ref, buf_ref, nxt_ref, sem):
    planes, nrows, cols = x_ref.shape
    members, points, _ = inner_ref.shape
    fields = points // nrows
    last = TOP + nrows
    load = pltpu.make_async_copy(x_ref, buf_ref.at[:, pl.ds(TOP, nrows), :], sem)
    load.start()
    compact(tile_ref, owner_ref, place_ref, field_ref, weight_ref, value_ref, error_ref,
            params_ref, slots_ref, mask_ref, vals_ref)
    for f in range(fields):
        smooth_strip_ref[f, 3:8, :] = smooth_ref[f, 0:5, :]
        smooth_strip_ref[f, 8:13, :] = smooth_ref[f, nrows - 5 : nrows, :]
    load.wait()
    for p in range(planes):
        strip_ref[p, 3:8, :] = buf_ref[p, TOP : TOP + 5, :]
        strip_ref[p, 8:13, :] = buf_ref[p, last - 5 : last, :]

    def member(m, carry):
        for g in range(nrows // 8):
            smooth = [smooth_ref[f, 8 * g : 8 * g + 8, :] for f in range(fields)]
            for f, v in enumerate(substep(buf_ref, cross_ref, smooth, m, TOP + 8 * g)):
                nxt_ref[m * fields + f, TOP + 8 * g : TOP + 8 * g + 8, :] = v
        for g in range(nrows // 8):
            smooth = [smooth_ref[f, 8 * g : 8 * g + 8, :] for f in range(fields)]
            for f, v in enumerate(substep(nxt_ref, cross_ref, smooth, m, TOP + 8 * g)):
                inner_ref[m, f * nrows + 8 * g : f * nrows + 8 * g + 8, :] = v
        return carry

    lax.fori_loop(0, members, member, 0, unroll=True)


def compact(tile_ref, owner_ref, place_ref, field_ref, weight_ref, value_ref, error_ref,
            params_ref, slots_ref, mask_ref, vals_ref):
    batches, _, count = owner_ref.shape
    chunks = count // LANES
    rows = batches * chunks
    mine = tile_ref[0]
    for b in range(batches):
        own = jnp.where(owner_ref[b] == mine, 1.0, 0.0)
        for j in range(chunks):
            mask_ref[b * chunks + j : b * chunks + j + 1, :] = own[:, j * LANES : (j + 1) * LANES]
    mask = mask_ref[...]
    mask16 = mask.astype(BF16)
    upper = jnp.where(iota((LANES, LANES), 0) <= iota((LANES, LANES), 1), 1.0, 0.0).astype(BF16)
    inside = dot_nn(mask16, upper)
    totals = dot_nn(mask16, jnp.ones((LANES, LANES), BF16)).astype(BF16)
    a, c = iota((rows, rows), 0), iota((rows, rows), 1)
    before = jnp.where((c < a) & ((c >= chunks) == (a >= chunks)), 1.0, 0.0).astype(BF16)
    rank = inside + dot_nn(before, totals) - 1.0
    slots = jnp.where(mask > 0.5, rank, -1.0).astype(jnp.int32)
    slots_ref[...] = slots
    for b in range(batches):
        place = place_ref[b : b + 1, :]
        row = ((place.astype(F32) + 0.5) * (1.0 / 255.0)).astype(jnp.int32)
        vals_ref[b, 0:1, :] = (field_ref[b : b + 1, :] * 32 + row).astype(F32)
        vals_ref[b, 1:2, :] = (place - row * 255).astype(F32)
        vals_ref[b, 2:6, :] = weight_ref[b]
        vals_ref[b, 6:7, :] = value_ref[b : b + 1, :]
        vals_ref[b, 7:8, :] = error_ref[b : b + 1, :]
        total = jnp.zeros((24, CAP), F32)
        for j in range(chunks):
            parts = split3(vals_ref[b, :, j * LANES : (j + 1) * LANES])
            total = total + dot_nt(
                jnp.concatenate([p.astype(F32) for p in parts], axis=0).astype(BF16),
                chosen_rows(slots, b * chunks + j),
            )
        params_ref[:, b * CAP : (b + 1) * CAP] = total[0:8] + total[8:16] + total[16:24]


def localize_kernel(slots_ref, near_ref, far_ref, out_ref):
    batches, tiles, _ = out_ref.shape
    slots = slots_ref[...]
    rows = slots.shape[0]
    chunks = rows // batches
    for b in range(batches):
        total = jnp.zeros((3 * tiles, CAP), F32)
        for j in range(chunks):
            at = pl.ds(b * chunks + j, tiles // 2, stride=rows)
            parts = split3(jnp.concatenate([near_ref[at, :], far_ref[at, :]], axis=0))
            total = total + dot_nt(
                jnp.concatenate(parts, axis=0), chosen_rows(slots, b * chunks + j)
            )
        out_ref[b] = total[:tiles] + total[tiles : 2 * tiles] + total[2 * tiles :]


TOP = 16


def forecast_kernel(tile_ref, cross_ref, inner_ref, strip_ref, smooth_strip_ref, first_ref,
                    second_ref, params_ref, out_ref, buf_ref, nxt_ref, sm_ref, fin_ref, u_ref, state_ref,
                    prior_ref, sems):
    members, points, cols = inner_ref.shape
    fields = smooth_strip_ref.shape[0]
    nrows = points // fields
    planes = members * fields
    fin_ref[...] = inner_ref[...]
    sm_ref[...] = smooth_strip_ref[...]
    even = tile_ref[0] % 2 == 0
    for p in range(planes + fields):
        first, second = first_ref[p], second_ref[p]
        above, below = jnp.where(even, second, first), jnp.where(even, first, second)
        if p < planes:
            buf_ref[p, 8:24, :] = strip_ref[p]
            buf_ref[p, 9:11, :] = above
            buf_ref[p, 21:23, :] = below
        else:
            sm_ref[p - planes, 2:3, :] = above[1:2]
            sm_ref[p - planes, 13:14, :] = below[0:1]

    def member(m, carry):
        for h in range(2):
            smooth = [sm_ref[f, 8 * h : 8 * h + 8, :] for f in range(fields)]
            for f, v in enumerate(substep(buf_ref, cross_ref, smooth, m, 8 + 8 * h)):
                nxt_ref[m * fields + f, 8 + 8 * h : 16 + 8 * h, :] = v
        for h in range(2):
            smooth = [sm_ref[f, 8 * h : 8 * h + 8, :] for f in range(fields)]
            for f, v in enumerate(substep(nxt_ref, cross_ref, smooth, m, 8 + 8 * h)):
                at = f * nrows + h * (nrows - 2)
                fin_ref[m, at : at + 2, :] = v[3:5]
        return carry

    lax.fori_loop(0, members, member, 0, unroll=True)

    halves = cols // LANES
    own_rows = members * fields * 8
    for g in range(nrows // 8):
        for h in range(halves):
            for m in range(members):
                for f in range(fields):
                    k = (m * fields + f) * 8
                    state_ref[g * halves + h, k : k + 8, :] = fin_ref[
                        m, f * nrows + 8 * g : f * nrows + 8 * g + 8, h * LANES : (h + 1) * LANES
                    ]
    send = pltpu.make_async_copy(state_ref, out_ref.at[:, pl.ds(0, own_rows), :], sems.at[0])
    send.start()

    slots = params_ref.shape[1]
    spot = params_ref[0:1, :].astype(jnp.int32)
    column = params_ref[1:2, :].astype(jnp.int32)
    cid = iota((cols, slots), 0)
    left = jnp.where(cid == column, 1.0, 0.0).astype(BF16)
    right = jnp.where(cid == column + 1, 1.0, 0.0).astype(BF16)
    choice = jnp.concatenate([left, right], axis=1)
    choice = jnp.concatenate([choice, choice], axis=0)
    parts = split3(fin_ref[...].reshape(members * points, cols))[:2]
    u_ref[...] = dot_nn(jnp.concatenate(parts, axis=1), choice)
    w = [params_ref[2 + k : 3 + k, :] for k in range(4)]
    acc = [jnp.zeros((8, slots), F32) for _ in range(members)]
    for i in range(points // 8):
        here = iota((8, slots), 0) + 8 * i
        at, under = here == spot, here == spot + 1
        a0 = jnp.where(at, w[0], 0.0) + jnp.where(under, w[2], 0.0)
        a1 = jnp.where(at, w[1], 0.0) + jnp.where(under, w[3], 0.0)
        for m in range(members):
            rows = slice(m * points + 8 * i, m * points + 8 * i + 8)
            acc[m] = acc[m] + a0 * u_ref[rows, 0:slots] + a1 * u_ref[rows, slots : 2 * slots]
    for m in range(members):
        row = jnp.sum(acc[m], axis=0, keepdims=True)
        for q in range(slots // LANES):
            piece = row[:, q * LANES : (q + 1) * LANES]
            for b in range(nrows // 8 * halves):
                prior_ref[b, q * members + m : q * members + m + 1, :] = piece
    held = slots // LANES * members
    send_priors = pltpu.make_async_copy(
        prior_ref, out_ref.at[:, pl.ds(own_rows, held), :], sems.at[1]
    )
    send_priors.start()
    send.wait()
    send_priors.wait()


def load_priors(got_ref, prior_ref, batch):
    groups, rows, _ = got_ref.shape
    total = prior_ref.shape[0]
    members = total // groups
    pieces = CAP // LANES
    first = rows - (2 - batch) * pieces * members
    for s in range(groups):
        for q in range(pieces):
            k = first + q * members
            prior_ref[s * members : (s + 1) * members, q * LANES : (q + 1) * LANES] = got_ref[
                s, k : k + members, :
            ]
    return prior_ref[...]


def distance(k):
    return sum(step for i, step in enumerate(STEPS) if (k >> i) & 1)


def partial_mixing(tile_ref, out_ref, prior, value, error, loc):
    members = prior.shape[0]
    tiles = loc.shape[0]
    mean = jnp.sum(prior, axis=0, keepdims=True) * (1.0 / members)
    spread = prior - mean
    variance = jnp.sum(spread * spread, axis=0, keepdims=True) * (1.0 / (members - 1))
    error = jnp.where(error > 0.0, error, 1.0)
    total = variance + error
    root = jnp.sqrt(total)
    gain = (value - mean) / total - spread / (root * (jnp.sqrt(error) + root))
    gain = gain * (1.0 / (members - 1))
    groups = members // 8
    high, low, _ = split3(jnp.concatenate([spread] * groups, axis=0))
    group_of = iota(high.shape, 0) // members
    left, right = [], []
    for k in range(groups):
        a = (loc[:, None, :] * gain[None, 8 * k : 8 * k + 8, :]).reshape(tiles * 8, loc.shape[1])
        a_high, a_low, _ = split3(a)
        b_high, b_low = [
            jnp.where(group_of == k, p.astype(F32), 0.0).astype(BF16) for p in (high, low)
        ]
        left += [a_high, a_low, a_high]
        right += [b_high, b_high, b_low]
    out = dot_nt(jnp.concatenate(left, axis=1), jnp.concatenate(right, axis=1))
    mine = tile_ref[0]
    for k in range(tiles):
        out_ref[mine ^ distance(k)] = out[8 * k : 8 * k + 8]


def unpack_mixing(packed, members):
    return jnp.concatenate(
        [packed[:, k * members : (k + 1) * members] for k in range(members // 8)], axis=0
    )


def first_kernel(tile_ref, pri_ref, params_ref, loc_ref, out_ref, prior_ref):
    value, error = params_ref[6:7, 0:CAP], params_ref[7:8, 0:CAP]
    partial_mixing(tile_ref, out_ref, load_priors(pri_ref, prior_ref, 0), value, error, loc_ref[0])


def second_kernel(tile_ref, w0_ref, pri_ref, params_ref, loc_ref, out_ref, prior_ref):
    prior = load_priors(pri_ref, prior_ref, 1)
    members = prior_ref.shape[0]
    w0 = unpack_mixing(jnp.sum(w0_ref[...], axis=0), members)
    mean = jnp.sum(prior, axis=0, keepdims=True) * (1.0 / members)
    prior = prior + dot_nn(w0, prior - mean, HI)
    value, error = params_ref[6:7, CAP : 2 * CAP], params_ref[7:8, CAP : 2 * CAP]
    partial_mixing(tile_ref, out_ref, prior, value, error, loc_ref[1])


def apply_kernel(w0_ref, w1_ref, got_ref, out_ref):
    groups, held, _ = out_ref.shape
    w0_sum, w1_sum = jnp.sum(w0_ref[...], axis=0), jnp.sum(w1_ref[...], axis=0)
    members = groups * 4
    own = members // groups
    fields = held // (own * 8)
    w0, w1 = unpack_mixing(w0_sum, members), unpack_mixing(w1_sum, members)
    inv = 1.0 / members
    w = w0 + w1 + dot_nn(w1, w0 - jnp.sum(w0, axis=0, keepdims=True) * inv, HI)
    w = w - jnp.sum(w, axis=1, keepdims=True) * inv
    size = members * 8
    pieces = jnp.concatenate([p.astype(F32) for p in split3(w)[:2]], axis=1).astype(BF16)
    tall = jnp.where(iota((size, members), 0) // 8 == iota((size, members), 1), 1.0, 0.0)
    wide = jnp.where(
        iota((2 * members, 2 * size), 1) // 8 == iota((2 * members, 2 * size), 0), 1.0, 0.0
    )
    big = dot_nn(dot_nn(tall.astype(BF16), pieces).astype(BF16), wide.astype(BF16))
    same = iota((size, 2 * size), 0) % 8 == iota((size, 2 * size), 1) % 8
    big = jnp.where(same, big, 0.0).astype(BF16)
    for f in range(fields):
        x = jnp.concatenate(
            [
                got_ref[s, (m * fields + f) * 8 : (m * fields + f) * 8 + 8, :]
                for s in range(groups)
                for m in range(own)
            ],
            axis=0,
        )
        high, low, _ = split3(x)
        y = dot_nn(big, jnp.concatenate([high, high], axis=0)) + dot_nn(big[:, :size], low)
        y = x + y
        for s in range(groups):
            for m in range(own):
                k = (m * fields + f) * 8
                n = (s * own + m) * 8
                out_ref[s, k : k + 8, :] = y[n : n + 8]


def place_kernel(x_ref, out_ref, sems):
    _, nrows, cols = out_ref.shape
    halves = cols // LANES
    copies = []
    for b in range(nrows // 8 * halves):
        g, h = b // halves, b % halves
        to = out_ref.at[:, pl.ds(8 * g, 8), pl.ds(h * LANES, LANES)]
        copies.append(pltpu.make_async_copy(x_ref.at[b], to, sems.at[b]))
        copies[-1].start()
    for copy in copies:
        copy.wait()


VM = pltpu.VMEM
PARAMS = pltpu.CompilerParams(vmem_limit_bytes=32 << 20)


def shaped(shape, dtype=F32):
    return jax.ShapeDtypeStruct(shape, dtype)


def swap(x, distance):
    count = lax.axis_size("dom")
    return lax.ppermute(x, "dom", [(i, i ^ distance) for i in range(count)])


def exchange(x, axis):
    return lax.all_to_all(x, axis, split_axis=0, concat_axis=0, tiled=False)


def on_device(x, smooth, cross, obs_tile, place, field, weights, values, error, loc):
    members, fields, nrows, cols = x.shape
    batches, count = place.shape
    tiles = lax.axis_size("dom")
    groups = lax.axis_size("mem")
    slots = batches * CAP
    mine = lax.axis_index("dom").astype(jnp.int32).reshape(1)
    smem = pl.BlockSpec(memory_space=pltpu.SMEM)
    vmem = pl.BlockSpec(memory_space=pltpu.VMEM)

    rows = batches * count // LANES
    held = loc.reshape(rows, LANES)
    held = jnp.concatenate([held, swap(held, STEPS[0])], axis=0)

    planes = members * fields
    hbm = pl.BlockSpec(memory_space=pltpu.HBM)
    x_hbm = pltpu.with_memory_space_constraint(x.reshape(planes, nrows, cols), pltpu.HBM)
    first, second, cross = pl.pallas_call(
        edge_kernel,
        out_shape=(
            shaped((planes + fields, 2, cols)),
            shaped((planes + fields, 2, cols)),
            shaped(cross.shape),
        ),
        in_specs=[smem] + [hbm] * 3,
        scratch_shapes=[
            VM((planes, 8, cols), F32),
            VM((planes, 8, cols), F32),
            VM((fields, 8, cols), F32),
            VM((fields, 8, cols), F32),
            pltpu.SemaphoreType.DMA((5,)),
        ],
        compiler_params=PARAMS,
        name="edges",
    )(
        mine,
        x_hbm,
        pltpu.with_memory_space_constraint(smooth, pltpu.HBM),
        pltpu.with_memory_space_constraint(cross, pltpu.HBM),
    )
    first = swap(first, 1)
    pairs = [(i, i + 1) for i in range(1, tiles - 1, 2)]
    second = lax.ppermute(second, "dom", pairs + [(b, a) for a, b in pairs])

    points = fields * nrows
    params, slot, inner, strip, smooth_strip = pl.pallas_call(
        interior_kernel,
        out_shape=(
            shaped((8, slots)),
            shaped((rows, LANES), jnp.int32),
            shaped((members, points, cols)),
            shaped((planes, 16, cols)),
            shaped((fields, 16, cols)),
        ),
        in_specs=[smem, smem, hbm] + [vmem] * 7,
        scratch_shapes=[
            VM((rows, LANES), F32),
            VM((batches, 8, count), F32),
            VM((planes, nrows + 32, cols), F32),
            VM((planes, nrows + 32, cols), F32),
            pltpu.SemaphoreType.DMA,
        ],
        compiler_params=PARAMS,
        name="interior",
    )(
        mine, cross, x_hbm, smooth, obs_tile.transpose(0, 2, 1), place,
        field, weights.transpose(0, 2, 1), values, error,
    )

    held, first, second, params = lax.optimization_barrier((held, first, second, params))
    held = jnp.concatenate([held, swap(held, STEPS[1])], axis=0)

    own_rows = members * fields * 8
    prior_rows = members * slots // LANES
    blocks = nrows // 8 * (cols // LANES)
    sent = pl.pallas_call(
        forecast_kernel,
        out_shape=shaped((blocks, own_rows + prior_rows, LANES)),
        in_specs=[smem] * 2 + [vmem] * 6,
        out_specs=hbm,
        scratch_shapes=[
            VM((planes, 32, cols), F32),
            VM((planes, 32, cols), F32),
            VM((fields, 16, cols), F32),
            VM((members, points, cols), F32),
            VM((members * points, 2 * slots), F32),
            VM((blocks, own_rows, LANES), F32),
            VM((blocks, prior_rows, LANES), F32),
            pltpu.SemaphoreType.DMA((2,)),
        ],
        compiler_params=PARAMS,
        name="forecast",
    )(mine, cross, inner, strip, smooth_strip, first, second, params)
    held, sent = lax.optimization_barrier((held, sent))
    got = exchange(sent, "mem")
    held = jnp.concatenate([held, swap(held, STEPS[2])], axis=0)

    loc_own = pl.pallas_call(
        localize_kernel,
        out_shape=shaped((batches, tiles, CAP)),
        compiler_params=PARAMS,
        name="localize",
    )(slot, held, swap(held, STEPS[3]))

    total = members * groups
    mix = dict(
        out_shape=shaped((tiles, total * total // LANES, LANES)),
        scratch_shapes=[VM((total, CAP), F32)],
        compiler_params=PARAMS,
    )
    w0 = pl.pallas_call(first_kernel, in_specs=[smem] + [vmem] * 3, name="first", **mix)(
        mine, got, params, loc_own
    )
    w0 = exchange(w0, "dom")
    w1 = pl.pallas_call(second_kernel, in_specs=[smem] + [vmem] * 4, name="second", **mix)(
        mine, w0, got, params, loc_own
    )
    w1 = exchange(w1, "dom")
    back = pl.pallas_call(
        apply_kernel,
        out_shape=shaped((groups, own_rows, LANES)),
        compiler_params=PARAMS,
        name="apply",
    )(w0, w1, got)
    back = exchange(back, "mem")
    back = pl.pallas_call(
        place_kernel,
        out_shape=shaped((planes, nrows, cols)),
        out_specs=hbm,
        scratch_shapes=[pltpu.SemaphoreType.DMA((blocks,))],
        compiler_params=PARAMS,
        name="place",
    )(back.reshape(blocks, planes, 8, LANES))
    return back.reshape(x.shape)


def solution(mesh):
    placed = (
        P("mem", None, "dom", None),
        P(None, "dom", None),
        P(),
        P(),
        P(),
        P(),
        P(),
        P(),
        P(),
        P(None, "dom", None),
    )
    return jax.shard_map(
        on_device,
        mesh=mesh,
        in_specs=placed,
        out_specs=P("mem", None, "dom", None),
        check_vma=False,
    )
```

```python
import jax
import jax.numpy as jnp
from jax import lax
from jax.experimental import pallas as pl
from jax.experimental.pallas import tpu as pltpu
from jax.sharding import PartitionSpec as P

F32 = jnp.float32
BF16 = jnp.bfloat16
HI = lax.Precision.HIGHEST
CAP = 256
LANES = 128
STEPS = (8,2,4,1)


def split3(values):
    high = values.astype(BF16)
    rest = values - high.astype(F32)
    middle = rest.astype(BF16)
    low = (rest - middle.astype(F32)).astype(BF16)
    return high, middle, low


def dot_nt(a, b, precision=None):
    return lax.dot_general(
        a, b, (((1,), (1,)), ((), ())), precision=precision, preferred_element_type=F32
    )


def dot_nn(a, b, precision=None):
    return lax.dot_general(
        a, b, (((1,), (0,)), ((), ())), precision=precision, preferred_element_type=F32
    )


def iota(shape, dim):
    return lax.broadcasted_iota(jnp.int32, shape, dim)


def chosen_rows(slots, row):
    here = slots[row : row + 1, :] == iota((CAP, LANES), 0)
    return jnp.where(here, 1.0, 0.0).astype(BF16)


def substep(src_ref, cross_ref, smooth, m, base):
    fields = len(smooth)
    cols = src_ref.shape[2]
    lane = iota((8, cols), 1)
    own = [src_ref[m * fields + f, base : base + 8, :] for f in range(fields)]
    result = []
    for f in range(fields):
        v = own[f]
        lap = src_ref[m * fields + f, base + 1 : base + 9, :]
        lap = lap + src_ref[m * fields + f, base - 1 : base + 7, :]
        lap = lap + jnp.where(lane == cols - 1, 0.0, pltpu.roll(v, cols - 1, 1))
        lap = lap + jnp.where(lane == 0, 0.0, pltpu.roll(v, 1, 1)) - 4.0 * v
        mixed = cross_ref[f, 0] * own[0]
        for g in range(1, fields):
            mixed = mixed + cross_ref[f, g] * own[g]
        result.append(v + smooth[f] * lap + mixed)
    return result


def edge_kernel(tile_ref, x_ref, smooth_ref, cross_ref, first_ref, second_ref, cross_out_ref,
                tail_x, head_x, tail_s, head_s, sems):
    planes, nrows, _ = x_ref.shape
    fields = smooth_ref.shape[0]
    top, bottom = pl.ds(0, 8), pl.ds(nrows - 8, 8)
    copies = [
        pltpu.make_async_copy(x_ref.at[:, bottom, :], tail_x, sems.at[0]),
        pltpu.make_async_copy(smooth_ref.at[:, bottom, :], tail_s, sems.at[1]),
        pltpu.make_async_copy(x_ref.at[:, top, :], head_x, sems.at[2]),
        pltpu.make_async_copy(smooth_ref.at[:, top, :], head_s, sems.at[3]),
        pltpu.make_async_copy(cross_ref, cross_out_ref, sems.at[4]),
    ]
    for copy in copies:
        copy.start()
    for copy in copies:
        copy.wait()
    even = tile_ref[0] % 2 == 0
    for p in range(planes + fields):
        if p < planes:
            tail, head = tail_x[p, 6:8, :], head_x[p, 0:2, :]
        else:
            tail, head = tail_s[p - planes, 6:8, :], head_s[p - planes, 0:2, :]
        first_ref[p] = jnp.where(even, tail, head)
        second_ref[p] = jnp.where(even, head, tail)


def interior_kernel(tile_ref, cross_ref, x_ref, smooth_ref, owner_ref, place_ref, field_ref,
                    weight_ref, value_ref, error_ref,
                    params_ref, slots_ref, inner_ref, strip_ref, smooth_strip_ref,
                    mask_ref, vals_ref, buf_ref, nxt_ref, sem):
    planes, nrows, cols = x_ref.shape
    members, points, _ = inner_ref.shape
    fields = points // nrows
    last = TOP + nrows
    load = pltpu.make_async_copy(x_ref, buf_ref.at[:, pl.ds(TOP, nrows), :], sem)
    load.start()
    compact(tile_ref, owner_ref, place_ref, field_ref, weight_ref, value_ref, error_ref,
            params_ref, slots_ref, mask_ref, vals_ref)
    for f in range(fields):
        smooth_strip_ref[f, 3:8, :] = smooth_ref[f, 0:5, :]
        smooth_strip_ref[f, 8:13, :] = smooth_ref[f, nrows - 5 : nrows, :]
    load.wait()
    for p in range(planes):
        strip_ref[p, 3:8, :] = buf_ref[p, TOP : TOP + 5, :]
        strip_ref[p, 8:13, :] = buf_ref[p, last - 5 : last, :]

    def member(m, carry):
        for g in range(nrows // 8):
            smooth = [smooth_ref[f, 8 * g : 8 * g + 8, :] for f in range(fields)]
            for f, v in enumerate(substep(buf_ref, cross_ref, smooth, m, TOP + 8 * g)):
                nxt_ref[m * fields + f, TOP + 8 * g : TOP + 8 * g + 8, :] = v
        for g in range(nrows // 8):
            smooth = [smooth_ref[f, 8 * g : 8 * g + 8, :] for f in range(fields)]
            for f, v in enumerate(substep(nxt_ref, cross_ref, smooth, m, TOP + 8 * g)):
                inner_ref[m, f * nrows + 8 * g : f * nrows + 8 * g + 8, :] = v
        return carry

    lax.fori_loop(0, members, member, 0, unroll=True)


def compact(tile_ref, owner_ref, place_ref, field_ref, weight_ref, value_ref, error_ref,
            params_ref, slots_ref, mask_ref, vals_ref):
    batches, _, count = owner_ref.shape
    chunks = count // LANES
    rows = batches * chunks
    mine = tile_ref[0]
    for b in range(batches):
        own = jnp.where(owner_ref[b] == mine, 1.0, 0.0)
        for j in range(chunks):
            mask_ref[b * chunks + j : b * chunks + j + 1, :] = own[:, j * LANES : (j + 1) * LANES]
    mask = mask_ref[...]
    mask16 = mask.astype(BF16)
    upper = jnp.where(iota((LANES, LANES), 0) <= iota((LANES, LANES), 1), 1.0, 0.0).astype(BF16)
    inside = dot_nn(mask16, upper)
    totals = dot_nn(mask16, jnp.ones((LANES, LANES), BF16)).astype(BF16)
    a, c = iota((rows, rows), 0), iota((rows, rows), 1)
    before = jnp.where((c < a) & ((c >= chunks) == (a >= chunks)), 1.0, 0.0).astype(BF16)
    rank = inside + dot_nn(before, totals) - 1.0
    slots = jnp.where(mask > 0.5, rank, -1.0).astype(jnp.int32)
    slots_ref[...] = slots
    for b in range(batches):
        place = place_ref[b : b + 1, :]
        row = ((place.astype(F32) + 0.5) * (1.0 / 255.0)).astype(jnp.int32)
        vals_ref[b, 0:1, :] = (field_ref[b : b + 1, :] * 32 + row).astype(F32)
        vals_ref[b, 1:2, :] = (place - row * 255).astype(F32)
        vals_ref[b, 2:6, :] = weight_ref[b]
        vals_ref[b, 6:7, :] = value_ref[b : b + 1, :]
        vals_ref[b, 7:8, :] = error_ref[b : b + 1, :]
        total = jnp.zeros((24, CAP), F32)
        for j in range(chunks):
            parts = split3(vals_ref[b, :, j * LANES : (j + 1) * LANES])
            total = total + dot_nt(
                jnp.concatenate([p.astype(F32) for p in parts], axis=0).astype(BF16),
                chosen_rows(slots, b * chunks + j),
            )
        params_ref[:, b * CAP : (b + 1) * CAP] = total[0:8] + total[8:16] + total[16:24]


def localize_kernel(slots_ref, near_ref, far_ref, out_ref):
    batches, tiles, _ = out_ref.shape
    slots = slots_ref[...]
    rows = slots.shape[0]
    chunks = rows // batches
    for b in range(batches):
        total = jnp.zeros((3 * tiles, CAP), F32)
        for j in range(chunks):
            at = pl.ds(b * chunks + j, tiles // 2, stride=rows)
            parts = split3(jnp.concatenate([near_ref[at, :], far_ref[at, :]], axis=0))
            total = total + dot_nt(
                jnp.concatenate(parts, axis=0), chosen_rows(slots, b * chunks + j)
            )
        out_ref[b] = total[:tiles] + total[tiles : 2 * tiles] + total[2 * tiles :]


TOP = 16


def forecast_kernel(tile_ref, cross_ref, inner_ref, strip_ref, smooth_strip_ref, first_ref,
                    second_ref, params_ref, out_ref, buf_ref, nxt_ref, sm_ref, fin_ref, u_ref, state_ref,
                    prior_ref, sems):
    members, points, cols = inner_ref.shape
    fields = smooth_strip_ref.shape[0]
    nrows = points // fields
    planes = members * fields
    fin_ref[...] = inner_ref[...]
    sm_ref[...] = smooth_strip_ref[...]
    even = tile_ref[0] % 2 == 0
    for p in range(planes + fields):
        first, second = first_ref[p], second_ref[p]
        above, below = jnp.where(even, second, first), jnp.where(even, first, second)
        if p < planes:
            buf_ref[p, 8:24, :] = strip_ref[p]
            buf_ref[p, 9:11, :] = above
            buf_ref[p, 21:23, :] = below
        else:
            sm_ref[p - planes, 2:3, :] = above[1:2]
            sm_ref[p - planes, 13:14, :] = below[0:1]

    def member(m, carry):
        for h in range(2):
            smooth = [sm_ref[f, 8 * h : 8 * h + 8, :] for f in range(fields)]
            for f, v in enumerate(substep(buf_ref, cross_ref, smooth, m, 8 + 8 * h)):
                nxt_ref[m * fields + f, 8 + 8 * h : 16 + 8 * h, :] = v
        for h in range(2):
            smooth = [sm_ref[f, 8 * h : 8 * h + 8, :] for f in range(fields)]
            for f, v in enumerate(substep(nxt_ref, cross_ref, smooth, m, 8 + 8 * h)):
                at = f * nrows + h * (nrows - 2)
                fin_ref[m, at : at + 2, :] = v[3:5]
        return carry

    lax.fori_loop(0, members, member, 0, unroll=True)

    halves = cols // LANES
    own_rows = members * fields * 8
    for g in range(nrows // 8):
        for h in range(halves):
            for m in range(members):
                for f in range(fields):
                    k = (m * fields + f) * 8
                    state_ref[g * halves + h, k : k + 8, :] = fin_ref[
                        m, f * nrows + 8 * g : f * nrows + 8 * g + 8, h * LANES : (h + 1) * LANES
                    ]
    send = pltpu.make_async_copy(state_ref, out_ref.at[:, pl.ds(0, own_rows), :], sems.at[0])
    send.start()

    slots = params_ref.shape[1]
    spot = params_ref[0:1, :].astype(jnp.int32)
    column = params_ref[1:2, :].astype(jnp.int32)
    cid = iota((cols, slots), 0)
    left = jnp.where(cid == column, 1.0, 0.0).astype(BF16)
    right = jnp.where(cid == column + 1, 1.0, 0.0).astype(BF16)
    choice = jnp.concatenate([left, right], axis=1)
    choice = jnp.concatenate([choice, choice], axis=0)
    parts = split3(fin_ref[...].reshape(members * points, cols))[:2]
    u_ref[...] = dot_nn(jnp.concatenate(parts, axis=1), choice)
    w = [params_ref[2 + k : 3 + k, :] for k in range(4)]
    acc = [jnp.zeros((8, slots), F32) for _ in range(members)]
    for i in range(points // 8):
        here = iota((8, slots), 0) + 8 * i
        at, under = here == spot, here == spot + 1
        a0 = jnp.where(at, w[0], 0.0) + jnp.where(under, w[2], 0.0)
        a1 = jnp.where(at, w[1], 0.0) + jnp.where(under, w[3], 0.0)
        for m in range(members):
            rows = slice(m * points + 8 * i, m * points + 8 * i + 8)
            acc[m] = acc[m] + a0 * u_ref[rows, 0:slots] + a1 * u_ref[rows, slots : 2 * slots]
    for m in range(members):
        row = jnp.sum(acc[m], axis=0, keepdims=True)
        for q in range(slots // LANES):
            piece = row[:, q * LANES : (q + 1) * LANES]
            for b in range(nrows // 8 * halves):
                prior_ref[b, q * members + m : q * members + m + 1, :] = piece
    held = slots // LANES * members
    send_priors = pltpu.make_async_copy(
        prior_ref, out_ref.at[:, pl.ds(own_rows, held), :], sems.at[1]
    )
    send_priors.start()
    send.wait()
    send_priors.wait()


def load_priors(got_ref, prior_ref, batch):
    groups, rows, _ = got_ref.shape
    total = prior_ref.shape[0]
    members = total // groups
    pieces = CAP // LANES
    first = rows - (2 - batch) * pieces * members
    for s in range(groups):
        for q in range(pieces):
            k = first + q * members
            prior_ref[s * members : (s + 1) * members, q * LANES : (q + 1) * LANES] = got_ref[
                s, k : k + members, :
            ]
    return prior_ref[...]


def distance(k):
    return sum(step for i, step in enumerate(STEPS) if (k >> i) & 1)


def partial_mixing(tile_ref, out_ref, prior, value, error, loc):
    members = prior.shape[0]
    tiles = loc.shape[0]
    mean = jnp.sum(prior, axis=0, keepdims=True) * (1.0 / members)
    spread = prior - mean
    variance = jnp.sum(spread * spread, axis=0, keepdims=True) * (1.0 / (members - 1))
    error = jnp.where(error > 0.0, error, 1.0)
    total = variance + error
    root = jnp.sqrt(total)
    gain = (value - mean) / total - spread / (root * (jnp.sqrt(error) + root))
    gain = gain * (1.0 / (members - 1))
    groups = members // 8
    high, low, _ = split3(jnp.concatenate([spread] * groups, axis=0))
    group_of = iota(high.shape, 0) // members
    left, right = [], []
    for k in range(groups):
        a = (loc[:, None, :] * gain[None, 8 * k : 8 * k + 8, :]).reshape(tiles * 8, loc.shape[1])
        a_high, a_low, _ = split3(a)
        b_high, b_low = [
            jnp.where(group_of == k, p.astype(F32), 0.0).astype(BF16) for p in (high, low)
        ]
        left += [a_high, a_low, a_high]
        right += [b_high, b_high, b_low]
    out = dot_nt(jnp.concatenate(left, axis=1), jnp.concatenate(right, axis=1))
    mine = tile_ref[0]
    for k in range(tiles):
        out_ref[mine ^ distance(k)] = out[8 * k : 8 * k + 8]


def unpack_mixing(packed, members):
    return jnp.concatenate(
        [packed[:, k * members : (k + 1) * members] for k in range(members // 8)], axis=0
    )


def first_kernel(tile_ref, pri_ref, params_ref, loc_ref, out_ref, prior_ref):
    value, error = params_ref[6:7, 0:CAP], params_ref[7:8, 0:CAP]
    partial_mixing(tile_ref, out_ref, load_priors(pri_ref, prior_ref, 0), value, error, loc_ref[0])


def second_kernel(tile_ref, w0_ref, pri_ref, params_ref, loc_ref, out_ref, prior_ref):
    prior = load_priors(pri_ref, prior_ref, 1)
    members = prior_ref.shape[0]
    w0 = unpack_mixing(jnp.sum(w0_ref[...], axis=0), members)
    mean = jnp.sum(prior, axis=0, keepdims=True) * (1.0 / members)
    prior = prior + dot_nn(w0, prior - mean, HI)
    value, error = params_ref[6:7, CAP : 2 * CAP], params_ref[7:8, CAP : 2 * CAP]
    partial_mixing(tile_ref, out_ref, prior, value, error, loc_ref[1])


def apply_kernel(w0_ref, w1_ref, got_ref, out_ref):
    groups, held, _ = out_ref.shape
    w0_sum, w1_sum = jnp.sum(w0_ref[...], axis=0), jnp.sum(w1_ref[...], axis=0)
    members = groups * 4
    own = members // groups
    fields = held // (own * 8)
    w0, w1 = unpack_mixing(w0_sum, members), unpack_mixing(w1_sum, members)
    inv = 1.0 / members
    w = w0 + w1 + dot_nn(w1, w0 - jnp.sum(w0, axis=0, keepdims=True) * inv, HI)
    w = w - jnp.sum(w, axis=1, keepdims=True) * inv
    size = members * 8
    pieces = jnp.concatenate([p.astype(F32) for p in split3(w)[:2]], axis=1).astype(BF16)
    tall = jnp.where(iota((size, members), 0) // 8 == iota((size, members), 1), 1.0, 0.0)
    wide = jnp.where(
        iota((2 * members, 2 * size), 1) // 8 == iota((2 * members, 2 * size), 0), 1.0, 0.0
    )
    big = dot_nn(dot_nn(tall.astype(BF16), pieces).astype(BF16), wide.astype(BF16))
    same = (iota((size, size), 0) - iota((size, size), 1)) & 7 == 0
    big_high, big_low = [
        jnp.where(same, big[:, k * size : (k + 1) * size], 0.0).astype(BF16) for k in range(2)
    ]
    big = jnp.concatenate([big_high, big_low, big_high], axis=1)
    for first in range(0, fields, 2):
        pair = range(first, min(first + 2, fields))
        x = jnp.concatenate(
            [
                jnp.concatenate(
                    [
                        got_ref[s, (m * fields + f) * 8 : (m * fields + f) * 8 + 8, :]
                        for s in range(groups)
                        for m in range(own)
                    ],
                    axis=0,
                )
                for f in pair
            ],
            axis=1,
        )
        high, low, _ = split3(x)
        y = x + dot_nn(big, jnp.concatenate([high, high, low], axis=0))
        for s in range(groups):
            for m in range(own):
                for f in pair:
                    k = (m * fields + f) * 8
                    n = (s * own + m) * 8
                    c = (f - first) * LANES
                    out_ref[s, k : k + 8, :] = y[n : n + 8, c : c + LANES]


def place_kernel(x_ref, out_ref, sems):
    _, nrows, cols = out_ref.shape
    halves = cols // LANES
    copies = []
    for b in range(nrows // 8 * halves):
        g, h = b // halves, b % halves
        to = out_ref.at[:, pl.ds(8 * g, 8), pl.ds(h * LANES, LANES)]
        copies.append(pltpu.make_async_copy(x_ref.at[b], to, sems.at[b]))
        copies[-1].start()
    for copy in copies:
        copy.wait()


VM = pltpu.VMEM
PARAMS = pltpu.CompilerParams(vmem_limit_bytes=32 << 20)


def shaped(shape, dtype=F32):
    return jax.ShapeDtypeStruct(shape, dtype)


def swap(x, distance):
    count = lax.axis_size("dom")
    return lax.ppermute(x, "dom", [(i, i ^ distance) for i in range(count)])


def exchange(x, axis):
    return lax.all_to_all(x, axis, split_axis=0, concat_axis=0, tiled=False)


def on_device(x, smooth, cross, obs_tile, place, field, weights, values, error, loc):
    members, fields, nrows, cols = x.shape
    batches, count = place.shape
    tiles = lax.axis_size("dom")
    groups = lax.axis_size("mem")
    slots = batches * CAP
    mine = lax.axis_index("dom").astype(jnp.int32).reshape(1)
    smem = pl.BlockSpec(memory_space=pltpu.SMEM)
    vmem = pl.BlockSpec(memory_space=pltpu.VMEM)

    rows = batches * count // LANES
    held = loc.reshape(rows, LANES)
    held = jnp.concatenate([held, swap(held, STEPS[0])], axis=0)

    planes = members * fields
    hbm = pl.BlockSpec(memory_space=pltpu.HBM)
    x_hbm = pltpu.with_memory_space_constraint(x.reshape(planes, nrows, cols), pltpu.HBM)
    first, second, cross = pl.pallas_call(
        edge_kernel,
        out_shape=(
            shaped((planes + fields, 2, cols)),
            shaped((planes + fields, 2, cols)),
            shaped(cross.shape),
        ),
        in_specs=[smem] + [hbm] * 3,
        scratch_shapes=[
            VM((planes, 8, cols), F32),
            VM((planes, 8, cols), F32),
            VM((fields, 8, cols), F32),
            VM((fields, 8, cols), F32),
            pltpu.SemaphoreType.DMA((5,)),
        ],
        compiler_params=PARAMS,
        name="edges",
    )(
        mine,
        x_hbm,
        pltpu.with_memory_space_constraint(smooth, pltpu.HBM),
        pltpu.with_memory_space_constraint(cross, pltpu.HBM),
    )
    first = swap(first, 1)
    pairs = [(i, i + 1) for i in range(1, tiles - 1, 2)]
    second = lax.ppermute(second, "dom", pairs + [(b, a) for a, b in pairs])

    points = fields * nrows
    params, slot, inner, strip, smooth_strip = pl.pallas_call(
        interior_kernel,
        out_shape=(
            shaped((8, slots)),
            shaped((rows, LANES), jnp.int32),
            shaped((members, points, cols)),
            shaped((planes, 16, cols)),
            shaped((fields, 16, cols)),
        ),
        in_specs=[smem, smem, hbm] + [vmem] * 7,
        scratch_shapes=[
            VM((rows, LANES), F32),
            VM((batches, 8, count), F32),
            VM((planes, nrows + 32, cols), F32),
            VM((planes, nrows + 32, cols), F32),
            pltpu.SemaphoreType.DMA,
        ],
        compiler_params=PARAMS,
        name="interior",
    )(
        mine, cross, x_hbm, smooth, obs_tile.transpose(0, 2, 1), place,
        field, weights.transpose(0, 2, 1), values, error,
    )

    held, first, second, params = lax.optimization_barrier((held, first, second, params))
    held = jnp.concatenate([held, swap(held, STEPS[1])], axis=0)

    own_rows = members * fields * 8
    prior_rows = members * slots // LANES
    blocks = nrows // 8 * (cols // LANES)
    sent = pl.pallas_call(
        forecast_kernel,
        out_shape=shaped((blocks, own_rows + prior_rows, LANES)),
        in_specs=[smem] * 2 + [vmem] * 6,
        out_specs=hbm,
        scratch_shapes=[
            VM((planes, 32, cols), F32),
            VM((planes, 32, cols), F32),
            VM((fields, 16, cols), F32),
            VM((members, points, cols), F32),
            VM((members * points, 2 * slots), F32),
            VM((blocks, own_rows, LANES), F32),
            VM((blocks, prior_rows, LANES), F32),
            pltpu.SemaphoreType.DMA((2,)),
        ],
        compiler_params=PARAMS,
        name="forecast",
    )(mine, cross, inner, strip, smooth_strip, first, second, params)
    held, sent = lax.optimization_barrier((held, sent))
    got = exchange(sent, "mem")
    held = jnp.concatenate([held, swap(held, STEPS[2])], axis=0)

    loc_own = pl.pallas_call(
        localize_kernel,
        out_shape=shaped((batches, tiles, CAP)),
        compiler_params=PARAMS,
        name="localize",
    )(slot, held, swap(held, STEPS[3]))

    total = members * groups
    mix = dict(
        out_shape=shaped((tiles, total * total // LANES, LANES)),
        scratch_shapes=[VM((total, CAP), F32)],
        compiler_params=PARAMS,
    )
    w0 = pl.pallas_call(first_kernel, in_specs=[smem] + [vmem] * 3, name="first", **mix)(
        mine, got, params, loc_own
    )
    w0 = exchange(w0, "dom")
    w1 = pl.pallas_call(second_kernel, in_specs=[smem] + [vmem] * 4, name="second", **mix)(
        mine, w0, got, params, loc_own
    )
    w1 = exchange(w1, "dom")
    back = pl.pallas_call(
        apply_kernel,
        out_shape=shaped((groups, own_rows, LANES)),
        compiler_params=PARAMS,
        name="apply",
    )(w0, w1, got)
    back = exchange(back, "mem")
    back = pl.pallas_call(
        place_kernel,
        out_shape=shaped((planes, nrows, cols)),
        out_specs=hbm,
        scratch_shapes=[pltpu.SemaphoreType.DMA((blocks,))],
        compiler_params=PARAMS,
        name="place",
    )(back.reshape(blocks, planes, 8, LANES))
    return back.reshape(x.shape)


def solution(mesh):
    placed = (
        P("mem", None, "dom", None),
        P(None, "dom", None),
        P(),
        P(),
        P(),
        P(),
        P(),
        P(),
        P(),
        P(None, "dom", None),
    )
    return jax.shard_map(
        on_device,
        mesh=mesh,
        in_specs=placed,
        out_specs=P("mem", None, "dom", None),
        check_vma=False,
    )
```

```python
import jax
import jax.numpy as jnp
from jax import lax
from jax.experimental import pallas as pl
from jax.experimental.pallas import tpu as pltpu
from jax.sharding import PartitionSpec as P

F32 = jnp.float32
BF16 = jnp.bfloat16
HI = lax.Precision.HIGHEST
CAP = 256
LANES = 128
STEPS = (8,2,4,1)


def split3(values):
    high = values.astype(BF16)
    rest = values - high.astype(F32)
    middle = rest.astype(BF16)
    low = (rest - middle.astype(F32)).astype(BF16)
    return high, middle, low


def dot_nt(a, b, precision=None):
    return lax.dot_general(
        a, b, (((1,), (1,)), ((), ())), precision=precision, preferred_element_type=F32
    )


def dot_nn(a, b, precision=None):
    return lax.dot_general(
        a, b, (((1,), (0,)), ((), ())), precision=precision, preferred_element_type=F32
    )


def iota(shape, dim):
    return lax.broadcasted_iota(jnp.int32, shape, dim)


def chosen_rows(slots, row):
    here = slots[row : row + 1, :] == iota((CAP, LANES), 0)
    return jnp.where(here, 1.0, 0.0).astype(BF16)


def substep(src_ref, cross_ref, smooth, m, base):
    fields = len(smooth)
    cols = src_ref.shape[2]
    lane = iota((8, cols), 1)
    own = [src_ref[m * fields + f, base : base + 8, :] for f in range(fields)]
    result = []
    for f in range(fields):
        v = own[f]
        lap = src_ref[m * fields + f, base + 1 : base + 9, :]
        lap = lap + src_ref[m * fields + f, base - 1 : base + 7, :]
        lap = lap + jnp.where(lane == cols - 1, 0.0, pltpu.roll(v, cols - 1, 1))
        lap = lap + jnp.where(lane == 0, 0.0, pltpu.roll(v, 1, 1)) - 4.0 * v
        mixed = cross_ref[f, 0] * own[0]
        for g in range(1, fields):
            mixed = mixed + cross_ref[f, g] * own[g]
        result.append(v + smooth[f] * lap + mixed)
    return result


def edge_kernel(tile_ref, x_ref, smooth_ref, cross_ref, first_ref, second_ref, cross_out_ref,
                tail_x, head_x, tail_s, head_s, sems):
    planes, nrows, _ = x_ref.shape
    fields = smooth_ref.shape[0]
    top, bottom = pl.ds(0, 8), pl.ds(nrows - 8, 8)
    copies = [
        pltpu.make_async_copy(x_ref.at[:, bottom, :], tail_x, sems.at[0]),
        pltpu.make_async_copy(smooth_ref.at[:, bottom, :], tail_s, sems.at[1]),
        pltpu.make_async_copy(x_ref.at[:, top, :], head_x, sems.at[2]),
        pltpu.make_async_copy(smooth_ref.at[:, top, :], head_s, sems.at[3]),
        pltpu.make_async_copy(cross_ref, cross_out_ref, sems.at[4]),
    ]
    for copy in copies:
        copy.start()
    for copy in copies:
        copy.wait()
    even = tile_ref[0] % 2 == 0
    for p in range(planes + fields):
        if p < planes:
            tail, head = tail_x[p, 6:8, :], head_x[p, 0:2, :]
        else:
            tail, head = tail_s[p - planes, 6:8, :], head_s[p - planes, 0:2, :]
        first_ref[p] = jnp.where(even, tail, head)
        second_ref[p] = jnp.where(even, head, tail)


def interior_kernel(tile_ref, cross_ref, x_ref, smooth_ref, owner_ref, place_ref, field_ref,
                    weight_ref, value_ref, error_ref,
                    params_ref, slots_ref, inner_ref, strip_ref, smooth_strip_ref,
                    mask_ref, vals_ref, buf_ref, nxt_ref, sem):
    planes, nrows, cols = x_ref.shape
    members, points, _ = inner_ref.shape
    fields = points // nrows
    last = TOP + nrows
    load = pltpu.make_async_copy(x_ref, buf_ref.at[:, pl.ds(TOP, nrows), :], sem)
    load.start()
    compact(tile_ref, owner_ref, place_ref, field_ref, weight_ref, value_ref, error_ref,
            params_ref, slots_ref, mask_ref, vals_ref)
    for f in range(fields):
        smooth_strip_ref[f, 3:8, :] = smooth_ref[f, 0:5, :]
        smooth_strip_ref[f, 8:13, :] = smooth_ref[f, nrows - 5 : nrows, :]
    load.wait()
    for p in range(planes):
        strip_ref[p, 3:8, :] = buf_ref[p, TOP : TOP + 5, :]
        strip_ref[p, 8:13, :] = buf_ref[p, last - 5 : last, :]

    def member(m, carry):
        for g in range(nrows // 8):
            smooth = [smooth_ref[f, 8 * g : 8 * g + 8, :] for f in range(fields)]
            for f, v in enumerate(substep(buf_ref, cross_ref, smooth, m, TOP + 8 * g)):
                nxt_ref[m * fields + f, TOP + 8 * g : TOP + 8 * g + 8, :] = v
        for g in range(nrows // 8):
            smooth = [smooth_ref[f, 8 * g : 8 * g + 8, :] for f in range(fields)]
            for f, v in enumerate(substep(nxt_ref, cross_ref, smooth, m, TOP + 8 * g)):
                inner_ref[m, f * nrows + 8 * g : f * nrows + 8 * g + 8, :] = v
        return carry

    lax.fori_loop(0, members, member, 0, unroll=True)


def compact(tile_ref, owner_ref, place_ref, field_ref, weight_ref, value_ref, error_ref,
            params_ref, slots_ref, mask_ref, vals_ref):
    batches, _, count = owner_ref.shape
    chunks = count // LANES
    rows = batches * chunks
    mine = tile_ref[0]
    for b in range(batches):
        own = jnp.where(owner_ref[b] == mine, 1.0, 0.0)
        for j in range(chunks):
            mask_ref[b * chunks + j : b * chunks + j + 1, :] = own[:, j * LANES : (j + 1) * LANES]
    mask = mask_ref[...]
    mask16 = mask.astype(BF16)
    upper = jnp.where(iota((LANES, LANES), 0) <= iota((LANES, LANES), 1), 1.0, 0.0).astype(BF16)
    inside = dot_nn(mask16, upper)
    totals = dot_nn(mask16, jnp.ones((LANES, LANES), BF16)).astype(BF16)
    a, c = iota((rows, rows), 0), iota((rows, rows), 1)
    before = jnp.where((c < a) & ((c >= chunks) == (a >= chunks)), 1.0, 0.0).astype(BF16)
    rank = inside + dot_nn(before, totals) - 1.0
    slots = jnp.where(mask > 0.5, rank, -1.0).astype(jnp.int32)
    slots_ref[...] = slots
    for b in range(batches):
        place = place_ref[b : b + 1, :]
        row = ((place.astype(F32) + 0.5) * (1.0 / 255.0)).astype(jnp.int32)
        vals_ref[b, 0:1, :] = (field_ref[b : b + 1, :] * 32 + row).astype(F32)
        vals_ref[b, 1:2, :] = (place - row * 255).astype(F32)
        vals_ref[b, 2:6, :] = weight_ref[b]
        vals_ref[b, 6:7, :] = value_ref[b : b + 1, :]
        vals_ref[b, 7:8, :] = error_ref[b : b + 1, :]
        total = jnp.zeros((24, CAP), F32)
        for j in range(chunks):
            parts = split3(vals_ref[b, :, j * LANES : (j + 1) * LANES])
            total = total + dot_nt(
                jnp.concatenate([p.astype(F32) for p in parts], axis=0).astype(BF16),
                chosen_rows(slots, b * chunks + j),
            )
        params_ref[:, b * CAP : (b + 1) * CAP] = total[0:8] + total[8:16] + total[16:24]


def localize_kernel(slots_ref, near_ref, far_ref, out_ref):
    batches, tiles, _ = out_ref.shape
    slots = slots_ref[...]
    rows = slots.shape[0]
    chunks = rows // batches
    for b in range(batches):
        total = jnp.zeros((3 * tiles, CAP), F32)
        for j in range(chunks):
            at = pl.ds(b * chunks + j, tiles // 2, stride=rows)
            parts = split3(jnp.concatenate([near_ref[at, :], far_ref[at, :]], axis=0))
            total = total + dot_nt(
                jnp.concatenate(parts, axis=0), chosen_rows(slots, b * chunks + j)
            )
        out_ref[b] = total[:tiles] + total[tiles : 2 * tiles] + total[2 * tiles :]


TOP = 16


def forecast_kernel(tile_ref, cross_ref, inner_ref, strip_ref, smooth_strip_ref, first_ref,
                    second_ref, params_ref, out_ref, buf_ref, nxt_ref, sm_ref, fin_ref, u_ref, state_ref,
                    prior_ref, sems):
    members, points, cols = inner_ref.shape
    fields = smooth_strip_ref.shape[0]
    nrows = points // fields
    planes = members * fields
    fin_ref[...] = inner_ref[...]
    sm_ref[...] = smooth_strip_ref[...]
    even = tile_ref[0] % 2 == 0
    for p in range(planes + fields):
        first, second = first_ref[p], second_ref[p]
        above, below = jnp.where(even, second, first), jnp.where(even, first, second)
        if p < planes:
            buf_ref[p, 8:24, :] = strip_ref[p]
            buf_ref[p, 9:11, :] = above
            buf_ref[p, 21:23, :] = below
        else:
            sm_ref[p - planes, 2:3, :] = above[1:2]
            sm_ref[p - planes, 13:14, :] = below[0:1]

    def member(m, carry):
        for h in range(2):
            smooth = [sm_ref[f, 8 * h : 8 * h + 8, :] for f in range(fields)]
            for f, v in enumerate(substep(buf_ref, cross_ref, smooth, m, 8 + 8 * h)):
                nxt_ref[m * fields + f, 8 + 8 * h : 16 + 8 * h, :] = v
        for h in range(2):
            smooth = [sm_ref[f, 8 * h : 8 * h + 8, :] for f in range(fields)]
            for f, v in enumerate(substep(nxt_ref, cross_ref, smooth, m, 8 + 8 * h)):
                at = f * nrows + h * (nrows - 2)
                fin_ref[m, at : at + 2, :] = v[3:5]
        return carry

    lax.fori_loop(0, members, member, 0, unroll=True)

    halves = cols // LANES
    own_rows = members * fields * 8
    for g in range(nrows // 8):
        for h in range(halves):
            for m in range(members):
                for f in range(fields):
                    k = (m * fields + f) * 8
                    state_ref[g * halves + h, k : k + 8, :] = fin_ref[
                        m, f * nrows + 8 * g : f * nrows + 8 * g + 8, h * LANES : (h + 1) * LANES
                    ]
    send = pltpu.make_async_copy(state_ref, out_ref.at[:, pl.ds(0, own_rows), :], sems.at[0])
    send.start()

    slots = params_ref.shape[1]
    spot = params_ref[0:1, :].astype(jnp.int32)
    column = params_ref[1:2, :].astype(jnp.int32)
    cid = iota((cols, slots), 0)
    left = jnp.where(cid == column, 1.0, 0.0).astype(BF16)
    right = jnp.where(cid == column + 1, 1.0, 0.0).astype(BF16)
    choice = jnp.concatenate([left, right], axis=1)
    choice = jnp.concatenate([choice, choice], axis=0)
    parts = split3(fin_ref[...].reshape(members * points, cols))[:2]
    u_ref[...] = dot_nn(jnp.concatenate(parts, axis=1), choice)
    w = [params_ref[2 + k : 3 + k, :] for k in range(4)]
    acc = [jnp.zeros((8, slots), F32) for _ in range(members)]
    for i in range(points // 8):
        here = iota((8, slots), 0) + 8 * i
        at, under = here == spot, here == spot + 1
        a0 = jnp.where(at, w[0], 0.0) + jnp.where(under, w[2], 0.0)
        a1 = jnp.where(at, w[1], 0.0) + jnp.where(under, w[3], 0.0)
        for m in range(members):
            rows = slice(m * points + 8 * i, m * points + 8 * i + 8)
            acc[m] = acc[m] + a0 * u_ref[rows, 0:slots] + a1 * u_ref[rows, slots : 2 * slots]
    for m in range(members):
        row = jnp.sum(acc[m], axis=0, keepdims=True)
        for q in range(slots // LANES):
            piece = row[:, q * LANES : (q + 1) * LANES]
            for b in range(nrows // 8 * halves):
                prior_ref[b, q * members + m : q * members + m + 1, :] = piece
    held = slots // LANES * members
    send_priors = pltpu.make_async_copy(
        prior_ref, out_ref.at[:, pl.ds(own_rows, held), :], sems.at[1]
    )
    send_priors.start()
    send.wait()
    send_priors.wait()


def load_priors(got_ref, prior_ref, batch):
    groups, rows, _ = got_ref.shape
    total = prior_ref.shape[0]
    members = total // groups
    pieces = CAP // LANES
    first = rows - (2 - batch) * pieces * members
    for s in range(groups):
        for q in range(pieces):
            k = first + q * members
            prior_ref[s * members : (s + 1) * members, q * LANES : (q + 1) * LANES] = got_ref[
                s, k : k + members, :
            ]
    return prior_ref[...]


def distance(k):
    return sum(step for i, step in enumerate(STEPS) if (k >> i) & 1)


def partial_mixing(tile_ref, out_ref, prior, value, error, loc):
    members = prior.shape[0]
    tiles = loc.shape[0]
    mean = jnp.sum(prior, axis=0, keepdims=True) * (1.0 / members)
    spread = prior - mean
    variance = jnp.sum(spread * spread, axis=0, keepdims=True) * (1.0 / (members - 1))
    error = jnp.where(error > 0.0, error, 1.0)
    total = variance + error
    root = jnp.sqrt(total)
    gain = (value - mean) / total - spread / (root * (jnp.sqrt(error) + root))
    gain = gain * (1.0 / (members - 1))
    groups = members // 8
    high, low, _ = split3(jnp.concatenate([spread] * groups, axis=0))
    group_of = iota(high.shape, 0) // members
    left, right = [], []
    for k in range(groups):
        a = (loc[:, None, :] * gain[None, 8 * k : 8 * k + 8, :]).reshape(tiles * 8, loc.shape[1])
        a_high, a_low, _ = split3(a)
        b_high, b_low = [
            jnp.where(group_of == k, p.astype(F32), 0.0).astype(BF16) for p in (high, low)
        ]
        left += [a_high, a_low, a_high]
        right += [b_high, b_high, b_low]
    out = dot_nt(jnp.concatenate(left, axis=1), jnp.concatenate(right, axis=1))
    mine = tile_ref[0]
    for k in range(tiles):
        out_ref[mine ^ distance(k)] = out[8 * k : 8 * k + 8]


def unpack_mixing(packed, members):
    return jnp.concatenate(
        [packed[:, k * members : (k + 1) * members] for k in range(members // 8)], axis=0
    )


def first_kernel(tile_ref, pri_ref, params_ref, loc_ref, out_ref, prior_ref):
    value, error = params_ref[6:7, 0:CAP], params_ref[7:8, 0:CAP]
    partial_mixing(tile_ref, out_ref, load_priors(pri_ref, prior_ref, 0), value, error, loc_ref[0])


def second_kernel(tile_ref, w0_ref, pri_ref, params_ref, loc_ref, out_ref, prior_ref):
    prior = load_priors(pri_ref, prior_ref, 1)
    members = prior_ref.shape[0]
    w0 = unpack_mixing(jnp.sum(w0_ref[...], axis=0), members)
    mean = jnp.sum(prior, axis=0, keepdims=True) * (1.0 / members)
    prior = prior + dot_nn(w0, prior - mean, HI)
    value, error = params_ref[6:7, CAP : 2 * CAP], params_ref[7:8, CAP : 2 * CAP]
    partial_mixing(tile_ref, out_ref, prior, value, error, loc_ref[1])


def apply_kernel(w0_ref, w1_ref, got_ref, out_ref):
    groups, held, _ = out_ref.shape
    w0_sum, w1_sum = jnp.sum(w0_ref[...], axis=0), jnp.sum(w1_ref[...], axis=0)
    members = groups * 4
    own = members // groups
    fields = held // (own * 8)
    w0, w1 = unpack_mixing(w0_sum, members), unpack_mixing(w1_sum, members)
    inv = 1.0 / members
    w = w0 + w1 + dot_nn(w1, w0 - jnp.sum(w0, axis=0, keepdims=True) * inv, HI)
    w = w - jnp.sum(w, axis=1, keepdims=True) * inv
    size = members * 8
    pieces = jnp.concatenate([p.astype(F32) for p in split3(w)[:2]], axis=1).astype(BF16)
    tall = jnp.where(iota((size, members), 0) // 8 == iota((size, members), 1), 1.0, 0.0)
    wide = jnp.where(
        iota((2 * members, 2 * size), 1) // 8 == iota((2 * members, 2 * size), 0), 1.0, 0.0
    )
    big = dot_nn(dot_nn(tall.astype(BF16), pieces).astype(BF16), wide.astype(BF16))
    same = (iota((size, size), 0) - iota((size, size), 1)) & 7 == 0
    big_high, big_low = [
        jnp.where(same, big[:, k * size : (k + 1) * size], 0.0).astype(BF16) for k in range(2)
    ]
    big = jnp.concatenate([big_high, big_low, big_high], axis=1)
    for first in range(0, fields, 2):
        pair = range(first, min(first + 2, fields))
        x = jnp.concatenate(
            [
                jnp.concatenate(
                    [
                        got_ref[s, (m * fields + f) * 8 : (m * fields + f) * 8 + 8, :]
                        for s in range(groups)
                        for m in range(own)
                    ],
                    axis=0,
                )
                for f in pair
            ],
            axis=1,
        )
        total = jnp.sum(x.reshape(members, 8, x.shape[1]), axis=0) * inv
        anomaly = x - jnp.concatenate([total] * members, axis=0)
        high, low, _ = split3(anomaly)
        y = x + dot_nn(big, jnp.concatenate([high, high, low], axis=0))
        for s in range(groups):
            for m in range(own):
                for f in pair:
                    k = (m * fields + f) * 8
                    n = (s * own + m) * 8
                    c = (f - first) * LANES
                    out_ref[s, k : k + 8, :] = y[n : n + 8, c : c + LANES]


def place_kernel(x_ref, out_ref, sems):
    _, nrows, cols = out_ref.shape
    halves = cols // LANES
    copies = []
    for b in range(nrows // 8 * halves):
        g, h = b // halves, b % halves
        to = out_ref.at[:, pl.ds(8 * g, 8), pl.ds(h * LANES, LANES)]
        copies.append(pltpu.make_async_copy(x_ref.at[b], to, sems.at[b]))
        copies[-1].start()
    for copy in copies:
        copy.wait()


VM = pltpu.VMEM
PARAMS = pltpu.CompilerParams(vmem_limit_bytes=32 << 20)


def shaped(shape, dtype=F32):
    return jax.ShapeDtypeStruct(shape, dtype)


def swap(x, distance):
    count = lax.axis_size("dom")
    return lax.ppermute(x, "dom", [(i, i ^ distance) for i in range(count)])


def exchange(x, axis):
    return lax.all_to_all(x, axis, split_axis=0, concat_axis=0, tiled=False)


def on_device(x, smooth, cross, obs_tile, place, field, weights, values, error, loc):
    members, fields, nrows, cols = x.shape
    batches, count = place.shape
    tiles = lax.axis_size("dom")
    groups = lax.axis_size("mem")
    slots = batches * CAP
    mine = lax.axis_index("dom").astype(jnp.int32).reshape(1)
    smem = pl.BlockSpec(memory_space=pltpu.SMEM)
    vmem = pl.BlockSpec(memory_space=pltpu.VMEM)

    rows = batches * count // LANES
    held = loc.reshape(rows, LANES)
    held = jnp.concatenate([held, swap(held, STEPS[0])], axis=0)

    planes = members * fields
    hbm = pl.BlockSpec(memory_space=pltpu.HBM)
    x_hbm = pltpu.with_memory_space_constraint(x.reshape(planes, nrows, cols), pltpu.HBM)
    first, second, cross = pl.pallas_call(
        edge_kernel,
        out_shape=(
            shaped((planes + fields, 2, cols)),
            shaped((planes + fields, 2, cols)),
            shaped(cross.shape),
        ),
        in_specs=[smem] + [hbm] * 3,
        scratch_shapes=[
            VM((planes, 8, cols), F32),
            VM((planes, 8, cols), F32),
            VM((fields, 8, cols), F32),
            VM((fields, 8, cols), F32),
            pltpu.SemaphoreType.DMA((5,)),
        ],
        compiler_params=PARAMS,
        name="edges",
    )(
        mine,
        x_hbm,
        pltpu.with_memory_space_constraint(smooth, pltpu.HBM),
        pltpu.with_memory_space_constraint(cross, pltpu.HBM),
    )
    first = swap(first, 1)
    pairs = [(i, i + 1) for i in range(1, tiles - 1, 2)]
    second = lax.ppermute(second, "dom", pairs + [(b, a) for a, b in pairs])

    points = fields * nrows
    params, slot, inner, strip, smooth_strip = pl.pallas_call(
        interior_kernel,
        out_shape=(
            shaped((8, slots)),
            shaped((rows, LANES), jnp.int32),
            shaped((members, points, cols)),
            shaped((planes, 16, cols)),
            shaped((fields, 16, cols)),
        ),
        in_specs=[smem, smem, hbm] + [vmem] * 7,
        scratch_shapes=[
            VM((rows, LANES), F32),
            VM((batches, 8, count), F32),
            VM((planes, nrows + 32, cols), F32),
            VM((planes, nrows + 32, cols), F32),
            pltpu.SemaphoreType.DMA,
        ],
        compiler_params=PARAMS,
        name="interior",
    )(
        mine, cross, x_hbm, smooth, obs_tile.transpose(0, 2, 1), place,
        field, weights.transpose(0, 2, 1), values, error,
    )

    held, first, second, params = lax.optimization_barrier((held, first, second, params))
    held = jnp.concatenate([held, swap(held, STEPS[1])], axis=0)

    own_rows = members * fields * 8
    prior_rows = members * slots // LANES
    blocks = nrows // 8 * (cols // LANES)
    sent = pl.pallas_call(
        forecast_kernel,
        out_shape=shaped((blocks, own_rows + prior_rows, LANES)),
        in_specs=[smem] * 2 + [vmem] * 6,
        out_specs=hbm,
        scratch_shapes=[
            VM((planes, 32, cols), F32),
            VM((planes, 32, cols), F32),
            VM((fields, 16, cols), F32),
            VM((members, points, cols), F32),
            VM((members * points, 2 * slots), F32),
            VM((blocks, own_rows, LANES), F32),
            VM((blocks, prior_rows, LANES), F32),
            pltpu.SemaphoreType.DMA((2,)),
        ],
        compiler_params=PARAMS,
        name="forecast",
    )(mine, cross, inner, strip, smooth_strip, first, second, params)
    held, sent = lax.optimization_barrier((held, sent))
    got = exchange(sent, "mem")
    held = jnp.concatenate([held, swap(held, STEPS[2])], axis=0)

    loc_own = pl.pallas_call(
        localize_kernel,
        out_shape=shaped((batches, tiles, CAP)),
        compiler_params=PARAMS,
        name="localize",
    )(slot, held, swap(held, STEPS[3]))

    total = members * groups
    mix = dict(
        out_shape=shaped((tiles, total * total // LANES, LANES)),
        scratch_shapes=[VM((total, CAP), F32)],
        compiler_params=PARAMS,
    )
    w0 = pl.pallas_call(first_kernel, in_specs=[smem] + [vmem] * 3, name="first", **mix)(
        mine, got, params, loc_own
    )
    w0 = exchange(w0, "dom")
    w1 = pl.pallas_call(second_kernel, in_specs=[smem] + [vmem] * 4, name="second", **mix)(
        mine, w0, got, params, loc_own
    )
    w1 = exchange(w1, "dom")
    back = pl.pallas_call(
        apply_kernel,
        out_shape=shaped((groups, own_rows, LANES)),
        compiler_params=PARAMS,
        name="apply",
    )(w0, w1, got)
    back = exchange(back, "mem")
    back = pl.pallas_call(
        place_kernel,
        out_shape=shaped((planes, nrows, cols)),
        out_specs=hbm,
        scratch_shapes=[pltpu.SemaphoreType.DMA((blocks,))],
        compiler_params=PARAMS,
        name="place",
    )(back.reshape(blocks, planes, 8, LANES))
    return back.reshape(x.shape)


def solution(mesh):
    placed = (
        P("mem", None, "dom", None),
        P(None, "dom", None),
        P(),
        P(),
        P(),
        P(),
        P(),
        P(),
        P(),
        P(None, "dom", None),
    )
    return jax.shard_map(
        on_device,
        mesh=mesh,
        in_specs=placed,
        out_specs=P("mem", None, "dom", None),
        check_vma=False,
    )
```
